32 devices in a mesh: groups: 2 (over x), stack: 4 (over y, core), bloch: 4 (over z).
Axes of the slice: x: 2, y: 2, z: 4, core: 2. Of those that a mesh axis runs over, the one named last changes fastest.
Arguments:
- drive: float32 [8, 8, 2, 192, 256], P(('groups', 'bloch'), 'stack'), parts along dimension 0, may hold values from -6 to 6
- positions: int32 [512], P('groups'), parts along dimension 0, may hold values from 0 to 3
- materials: int32 [16], P(('groups', 'stack')), parts along dimension 0, may hold values from 0 to 3
- table: float32 [4, 4, 192, 192], replicated, may hold values from -1 to 1
- thickness: float32 [16], P(('groups', 'stack')), parts along dimension 0, may hold values from 0.25 to 4
- decay: float32 [192], replicated, may hold values from 0.0025 to 2
Outputs:
- up_field: float32 [8, 4, 192, 256], P(('groups', 'bloch'), 'stack'), parts along dimension 0
- down_field: float32 [8, 4, 192, 256], P(('groups', 'bloch'), 'stack'), parts along dimension 0
The draws below stay inside these ranges and needn't reach their ends.
There are 2 independent parts, one for each index of `groups`. The reference program is written for one: setup_inputs(seed, part) draws one part's arguments, and reference() takes and returns one part's arrays. A program takes and returns all parts, laid end to end along the dimension named above; an argument that names none is the same for every part. Nothing has to cross between parts.
All inputs are finite; a program needn't handle non-finite values.
Results may differ from the reference program's by a relative error of at most 0.00013.
Values sent between devices are 32-bit elements; how exact they have to be, the bound alone decides.
No kernel may reach another device: no remote copies, remote signals or barrier semaphores. Data moves between devices by JAX's collectives and lax.ppermute only.
A program may use at most 64 MiB of HBM per device.

```python
import math
import jax
import jax.numpy as jnp
from jax import lax

MODES = 192
COLS = 256
SLAB = 2
MATERIALS = 4
CELLS = 4
LAYERS = 8
SLABS = 4


def draw_table(key, part):
    key_refl = jax.random.fold_in(key, 11)
    key_couple = jax.random.fold_in(key, 23)
    key_diag = jax.random.fold_in(key, 37)
    couplings = jax.random.normal(key_couple, (MATERIALS, 2, MODES, MODES), jnp.float32) * (0.25 / math.sqrt(MODES))
    reflections = jax.random.normal(key_refl, (MATERIALS, 2, MODES, MODES), jnp.float32) * (0.3 / math.sqrt(MODES))
    diagonal = jax.random.uniform(key_diag, (MATERIALS, 2, MODES), jnp.float32, 0.7, 0.97)
    transmissions = couplings + diagonal[..., None] * jnp.eye(MODES, dtype=jnp.float32)
    blocks = jnp.stack([reflections[:, 0], transmissions[:, 0], transmissions[:, 1], reflections[:, 1]], axis=1)
    return jnp.clip(blocks, -1.0, 1.0)


def place_ends(entries, rng, smallest, top_value):
    extent = entries.shape
    spot = [jax.random.randint(jax.random.fold_in(rng, axis), (), 0, extent[axis]) for axis in range(len(extent))]
    entries = entries.at[tuple(spot)].set(smallest)
    longest = extent.index(max(extent))
    spot[longest] = (spot[longest] + 1) % extent[longest]
    return entries.at[tuple(spot)].set(top_value)


def levels(own_key, dims, split, low, top_value):
    def one(position, shards_of):
        draws = jax.random.uniform(jax.random.fold_in(jax.random.fold_in(own_key, 6), position), (shards_of,), jnp.float32, low / len(split), top_value / len(split))
        return jnp.repeat(jnp.exp(draws), dims[position] // shards_of).reshape((-1,) + (1,) * (len(dims) - position - 1))

    level = one(*split[0])
    for cut in split[1:]:
        level = level * one(*cut)
    return level


def normal_values(rng, extent, deviation, bound, pieces=(), kind=jnp.bfloat16):
    loudness = levels(rng, extent, pieces, -0.22, 0.18) if pieces else 1.0
    array = jax.random.normal(rng, extent, jnp.float32) * deviation * loudness
    return jnp.minimum(jnp.maximum(array, -bound), bound).astype(kind)


def setup_inputs(seed: int = 0, part: int = 0) -> dict:
    splits = jax.random.split(jax.random.key(seed), 7)
    part_splits = jax.random.split(jax.random.fold_in(splits[6], part), 7)
    return {
        "drive": normal_values(part_splits[0], (CELLS, LAYERS, 2, MODES, COLS), 1.0, 6.0, ((0, 4), (1, 4)), jnp.float32),
        "positions": place_ends(jax.random.randint(part_splits[1], (COLS,), 0, CELLS), jax.random.fold_in(part_splits[1], 1), 0, CELLS - 1).astype(jnp.int32),
        "materials": place_ends(jax.random.randint(part_splits[2], (LAYERS,), 0, MATERIALS), jax.random.fold_in(part_splits[2], 1), 0, MATERIALS - 1).astype(jnp.int32),
        "table": draw_table(jax.random.fold_in(splits[6], 71), part),
        "thickness": jnp.clip(jnp.exp(math.log(4.0) - 2.7725887 * jax.random.uniform(part_splits[4], (LAYERS,), jnp.float32) ** levels(part_splits[4], (LAYERS,), ((0, 4),), -0.2, 0.2)), 0.25, 4.0),
        "decay": jnp.clip(jnp.exp(jax.random.uniform(splits[5], (MODES,), jnp.float32, math.log(0.0025), math.log(2.0))), 0.0025, 2.0),
    }


precise = lax.Precision.HIGHEST

def product(left_side, right_side):
    return jnp.einsum('...ij,...jk->...ik', left_side, right_side, precision=precise)

def cas_table(cell_count):
    indices = jnp.arange(cell_count).astype(jnp.int32)
    phases = indices[:, None] * indices[None, :] % cell_count
    angles = phases.astype(jnp.float32) * (2.0 * math.pi / cell_count)
    return (jnp.cos(angles) + jnp.sin(angles)) / math.sqrt(cell_count)

def inverse_gap(coupling):
    identity = jnp.eye(coupling.shape[-1], dtype=coupling.dtype)
    system = identity - coupling
    return jnp.linalg.solve(system, jnp.broadcast_to(identity, system.shape))

def forward_join(above_part, below_part):
    refl_bot_a, src_down_a = above_part
    refl_top_b, trans_down_b, trans_up_b, refl_bot_b, src_up_b, src_down_b = below_part
    gap_inverse = inverse_gap(product(refl_bot_a, refl_top_b))
    down_inner = product(trans_down_b, gap_inverse)
    new_refl = refl_bot_b + product(down_inner, product(refl_bot_a, trans_up_b))
    new_source = src_down_b + product(down_inner, src_down_a + product(refl_bot_a, src_up_b))
    return (new_refl, new_source)

def backward_join(above_part, below_part):
    refl_top_a, trans_down_a, trans_up_a, refl_bot_a, src_up_a, src_down_a = above_part
    refl_top_b, src_up_b = below_part
    gap_inverse = inverse_gap(product(refl_bot_a, refl_top_b))
    reflect_inner = product(refl_top_b, gap_inverse)
    new_refl = refl_top_a + product(trans_up_a, product(reflect_inner, trans_down_a))
    crossing = product(gap_inverse, src_down_a + product(refl_bot_a, src_up_b))
    new_source = src_up_a + product(trans_up_a, product(refl_top_b, crossing) + src_up_b)
    return (new_refl, new_source)

def crossing_down(above_part, below_part):
    refl_bot_a, src_down_a = above_part
    refl_top_b, src_up_b = below_part
    gap_inverse = inverse_gap(product(refl_bot_a, refl_top_b))
    return product(gap_inverse, src_down_a + product(refl_bot_a, src_up_b))

def reference(drive, positions, materials, table, thickness, decay):
    cells = jnp.arange(CELLS).astype(jnp.int32)
    offset = jnp.abs(cells[:, None] - positions[None, :])
    offset = jnp.minimum(offset, CELLS - offset)
    envelope = 1.0 / (1.0 + offset.astype(jnp.float32))
    sources = drive * envelope[:, None, None, None, :]
    cas = cas_table(CELLS)
    spectrum = jnp.einsum('kc,clsme->klsme', cas, sources, precision=precise)
    waves = jnp.arange(CELLS).astype(jnp.float32)
    rates = decay[None, :] * (1.0 + 0.5 * jnp.cos(waves * (2.0 * math.pi / CELLS)))[:, None]
    chosen = table[materials]

    def element(layer_index):
        damping = jnp.exp(-thickness[layer_index] * rates)
        blocks = [damping[:, :, None] * chosen[layer_index, which][None] * damping[:, None, :] for which in range(4)]
        return (blocks[0], blocks[1], blocks[2], blocks[3], spectrum[:, layer_index, 0], spectrum[:, layer_index, 1])
    zero_matrix = jnp.zeros((CELLS, MODES, MODES), jnp.float32)
    zero_source = jnp.zeros((CELLS, MODES, COLS), jnp.float32)
    prefix = (zero_matrix, zero_source)
    tops = []
    bottoms = []
    for layer_index in range(LAYERS):
        if layer_index % SLAB == 0:
            tops.append(prefix)
        prefix = forward_join(prefix, element(layer_index))
        if layer_index % SLAB == SLAB - 1:
            bottoms.append(prefix)
    suffix = (zero_matrix, zero_source)
    below_list = [None] * SLABS
    from_list = [None] * SLABS
    for layer_index in range(LAYERS - 1, -1, -1):
        if layer_index % SLAB == SLAB - 1:
            below_list[layer_index // SLAB] = suffix
        suffix = backward_join(element(layer_index), suffix)
        if layer_index % SLAB == 0:
            from_list[layer_index // SLAB] = suffix
    up_list = []
    down_list = []
    for slab_index in range(SLABS):
        downward = crossing_down(tops[slab_index], from_list[slab_index])
        up_list.append(product(from_list[slab_index][0], downward) + from_list[slab_index][1])
        down_list.append(crossing_down(bottoms[slab_index], below_list[slab_index]))
    up_spec = jnp.stack(up_list, axis=1)
    down_spec = jnp.stack(down_list, axis=1)
    up_field = jnp.einsum('ck,ksme->csme', cas, up_spec, precision=precise)
    down_field = jnp.einsum('ck,ksme->csme', cas, down_spec, precision=precise)
    return (up_field, down_field)
```

```python
import functools
import math

import jax
import jax.numpy as jnp
from jax import lax
from jax.experimental import pallas as pl
from jax.experimental.pallas import tpu as pltpu
from jax.sharding import PartitionSpec as P

PAIR = 2
FIXED_DOUBLINGS = 3
SMALL = 3e-8

f32 = jnp.float32


def dot(left_side, right_side, precision=lax.Precision.HIGH):
    return lax.dot_general(
        left_side,
        right_side,
        (((1,), (0,)), ((), ())),
        precision=precision,
        preferred_element_type=f32,
    )


def eye(size):
    rows = lax.broadcasted_iota(jnp.int32, (size, size), 0)
    columns = lax.broadcasted_iota(jnp.int32, (size, size), 1)
    return (rows == columns).astype(f32)


def peak(value):
    return jnp.max(jnp.abs(value))


def inverses(couplings, sum_ref, power_ref, coupling_ref):
    size = couplings[0].shape[0]
    identity = eye(size)
    sums = [identity + c for c in couplings]
    powers = [dot(c, c) for c in couplings]
    for _ in range(FIXED_DOUBLINGS):
        sums = [s + dot(s, p) for s, p in zip(sums, powers)]
        powers = [dot(p, p) for p in powers]
    biggest = powers[0]
    biggest = jnp.abs(biggest)
    for p in powers[1:]:
        biggest = jnp.maximum(biggest, jnp.abs(p))
    for i, (s, p, c) in enumerate(zip(sums, powers, couplings)):
        sum_ref[i] = s
        power_ref[i] = p
        coupling_ref[i] = c
    worst = jnp.max(biggest)

    @pl.when(jnp.logical_not(worst <= SMALL))
    def _():
        def one(i, carry):
            def going(state):
                count, size_now = state
                return (count < 16) & (size_now > SMALL) & (size_now < 1e8)

            def double(state):
                count, _ = state
                power = power_ref[i]
                sum_ref[i] = sum_ref[i] + dot(sum_ref[i], power, lax.Precision.HIGHEST)
                power = dot(power, power, lax.Precision.HIGHEST)
                power_ref[i] = power
                return (count + 1, peak(power))

            _, left_over = lax.while_loop(going, double, (jnp.int32(0), peak(power_ref[i])))

            @pl.when(jnp.logical_not(left_over <= SMALL))
            def _():
                identity = eye(size)
                system = identity - coupling_ref[i]
                flipped = lax.dot_general(
                    system,
                    identity,
                    (((0,), (0,)), ((), ())),
                    precision=lax.Precision.HIGHEST,
                    preferred_element_type=f32,
                )
                row_bound = jnp.max(jnp.sum(jnp.abs(system), axis=1, keepdims=True))
                column_bound = jnp.max(jnp.sum(jnp.abs(system), axis=0, keepdims=True))
                sum_ref[i] = flipped / (row_bound * column_bound)

                def refining(state):
                    count, gap = state
                    return (count < 100) & (gap > 1e-4)

                def refine(state):
                    count, _ = state
                    system = eye(size) - coupling_ref[i]
                    error = eye(size) - dot(system, sum_ref[i], lax.Precision.HIGHEST)
                    sum_ref[i] = sum_ref[i] + dot(sum_ref[i], error, lax.Precision.HIGHEST)
                    return (count + 1, peak(error))

                lax.while_loop(refining, refine, (jnp.int32(0), f32(1.0)))

            return carry

        lax.fori_loop(0, len(couplings), one, 0)

    return [sum_ref[i] for i in range(len(couplings))]


def inner_maps(above, below, gap):
    _, _, up_a, bottom_a = above
    top_b, down_b, _, _ = below
    identity = eye(gap.shape[0])
    mid_y_d = dot(top_b, gap)
    mid_x_u = dot(gap, bottom_a)
    mid_y_u = identity + dot(top_b, mid_x_u)
    return (
        (dot(up_a, mid_y_d), gap, mid_y_d, dot(down_b, gap)),
        (dot(up_a, mid_y_u), mid_x_u, mid_y_u, dot(down_b, mid_x_u)),
    )


def in_batches(count, work):
    size = 2 if count % 2 == 0 else 1
    if count == size:
        work(0, size)
    else:
        def step(i, carry):
            work(i * size, size)
            return carry

        lax.fori_loop(0, count // size, step, 0)


def matrices_kernel(layers, vectors, *refs):
    in_batches(vectors, lambda start, size: matrices_of(layers, start, size, *refs))


def matrices_of(layers, start, vectors, factor_ref, material_ref, thick_ref, first_ref, table_ref, row_ref, column_ref,
                    slab_d, slab_u, pair_d, pair_u, end_x, end_y, onward, sum_ref, power_ref, coupling_ref):
    m = table_ref.shape[-1]
    segments = {}
    for k in range(vectors):
        for j in range(PAIR):
            for i in range(layers):
                thick = thick_ref[j * layers + i]
                which = material_ref[j * layers + i]
                row = jnp.exp(-(thick * factor_ref[start + k]) * row_ref[...])
                column = jnp.exp(-(thick * factor_ref[start + k]) * column_ref[...])
                segments[k, j, i] = tuple(column * table_ref[which, b] * row for b in range(4))
    slabs = {}
    keys = [(k, j) for k in range(vectors) for j in range(PAIR)]
    for k, j in keys:
        slabs[k, j] = segments[k, j, 0]
    for i in range(1, layers):
        gaps = inverses([dot(slabs[k, j][3], segments[k, j, i][0]) for k, j in keys], sum_ref, power_ref, coupling_ref)
        for (k, j), gap in zip(keys, gaps):
            above, below = slabs[k, j], segments[k, j, i]
            by_d, by_u = inner_maps(above, below, gap)
            slab_d[start + k, j, i - 1, 0:m] = by_d[0]
            slab_d[start + k, j, i - 1, m:] = by_d[3]
            slab_u[start + k, j, i - 1, 0:m] = by_u[0]
            slab_u[start + k, j, i - 1, m:] = by_u[3]
            slabs[k, j] = (
                above[0] + dot(by_d[0], above[1]),
                dot(by_d[3], above[1]),
                dot(by_u[0], below[2]),
                below[3] + dot(by_u[3], below[2]),
            )
    gaps = inverses([dot(slabs[k, 0][3], slabs[k, 1][0]) for k in range(vectors)], sum_ref, power_ref, coupling_ref)
    first = first_ref[0]
    for k, gap in zip(range(vectors), gaps):
        above, below = slabs[k, 0], slabs[k, 1]
        by_d, by_u = inner_maps(above, below, gap)
        top_x = above[0] + dot(by_d[0], above[1])
        end_y_end = below[3] + dot(by_u[3], below[2])
        onward[start + k] = jnp.where(first == 1, end_y_end, top_x)
        for r in range(4):
            pair_d[start + k, r * m:(r + 1) * m] = by_d[r]
            pair_u[start + k, r * m:(r + 1) * m] = by_u[r]
        end_x[start + k, 0:m] = top_x
        end_y[start + k, 0:m] = dot(by_u[0], below[2])
        for r in range(1, 4):
            end_x[start + k, r * m:(r + 1) * m] = dot(by_d[r], above[1])
        for r in range(1, 3):
            end_y[start + k, r * m:(r + 1) * m] = dot(by_u[r], below[2])
        end_y[start + k, 3 * m:] = end_y_end


def boundary_kernel(vectors, *refs):
    in_batches(vectors, lambda start, size: boundary_of(start, size, *refs))


def boundary_of(start, vectors, flag_ref, end_x, end_y, prefix_ref, suffix_ref, from_d, from_u, own_d, own_u,
                sum_ref, power_ref, coupling_ref):
    m = end_x.shape[-1]
    ks = [start + i for i in range(vectors)]
    prefix = [prefix_ref[k] * flag_ref[0] for k in ks]
    suffix = [suffix_ref[k] * flag_ref[1] for k in ks]
    lower = inverses([dot(s, end_y[k, 3 * m:]) for k, s in zip(ks, suffix)], sum_ref, power_ref, coupling_ref)
    bounced = [dot(dot(low, s), end_x[k, 3 * m:]) for k, low, s in zip(ks, lower, suffix)]
    top = [end_x[k, 0:m] + dot(end_y[k, 0:m], b) for k, b in zip(ks, bounced)]
    upper = inverses([dot(p, t) for p, t in zip(prefix, top)], sum_ref, power_ref, coupling_ref)
    for k, low, up, bounce, p, s in zip(ks, lower, upper, bounced, prefix, suffix):
        by_d = dot(end_x[k] + dot(end_y[k], bounce), up)
        by_u = dot(dot(by_d, dot(p, end_y[k, 0:m])) + end_y[k], low)
        from_d[k] = by_d
        from_u[k] = by_u
        own_u[k] = dot(by_d, p)
        own_d[k] = dot(by_u, s)


def pack_kernel(share, parts, where_ref, drive_ref, position_ref, *outs):
    *blocks, held = outs
    cell, cells = where_ref[0], parts
    offset = jnp.abs(cell - position_ref[...])
    offset = jnp.minimum(offset, cells - offset)
    envelope = 1.0 / (1.0 + offset.astype(f32))
    layers = drive_ref.shape[1]
    for q in range(parts):
        span = slice(q * share, (q + 1) * share)
        held[q] = jnp.concatenate(
            [drive_ref[0, i, d, :, span] * envelope[:, span] for i in range(layers) for d in range(2)], axis=1
        )
    for shift in range(parts):
        blocks[shift][...] = held[lax.rem(cell + shift, cells)]


def transform_kernel(parts, weight_ref, *refs):
    blocks, (kept, sent) = refs[:parts], refs[parts:]
    loaded = [b[...] for b in blocks]
    for side, out in enumerate((kept, sent)):
        for i in range(out.shape[0]):
            total = weight_ref[side, i, 0] * loaded[0]
            for shift in range(1, parts):
                total = total + weight_ref[side, i, shift] * loaded[shift]
            out[i] = total


def sources_kernel(layers, share, vectors, parity_ref, kept, got, slab_d, slab_u, pair_d, pair_u, inner, ends, held):
    m = kept.shape[1]
    parity = parity_ref[0]
    for k in range(vectors):
        held[parity, k] = kept[k]
        held[1 - parity, k] = got[k]
    for k in range(vectors):
        pair = []
        for j in range(PAIR):
            block = held[j, k]
            up, down = block[:, 0:share], block[:, share:2 * share]
            for i in range(1, layers):
                at = 2 * i * share
                up_b, down_b = block[:, at:at + share], block[:, at + share:at + 2 * share]
                both = dot(slab_d[k, j, i - 1], down) + dot(slab_u[k, j, i - 1], up_b)
                up, down = up + both[0:m], down_b + both[m:]
            pair.append((up, down))
        rows = dot(pair_d[k], pair[0][1]) + dot(pair_u[k], pair[1][0])
        top = rows[0:m] + pair[0][0]
        end = rows[3 * m:] + pair[1][1]
        inner[k, 0:m] = top
        inner[k, m:3 * m] = rows[m:3 * m]
        inner[k, 3 * m:] = end
        ends[k, 0] = end
        ends[k, 1] = top


def own_kernel(vectors, inner, ends, own_d, own_u, out):
    for k in range(vectors):
        out[k] = inner[k] + dot(own_d[k], ends[k, 0]) + dot(own_u[k], ends[k, 1])


def fields_kernel(vectors, flag_ref, parity_ref, inner, above_ref, below_ref, from_d, from_u, kept, sent, held):
    m = inner.shape[1] // 4
    for k in range(vectors):
        rows = inner[k] + dot(from_d[k], above_ref[k] * flag_ref[0]) + dot(from_u[k], below_ref[k] * flag_ref[1])
        for j in range(PAIR):
            held[j, k] = jnp.concatenate([rows[2 * j * m:(2 * j + 1) * m], rows[(2 * j + 1) * m:(2 * j + 2) * m]], axis=1)
    parity = parity_ref[0]
    for k in range(vectors):
        kept[k] = held[parity, k]
        sent[k] = held[1 - parity, k]


def return_kernel(parts, weight_ref, kept, got, *blocks):
    vectors = kept.shape[0]
    for shift in range(parts):
        total = weight_ref[0, 0, shift] * kept[0]
        for side, ref in enumerate((kept, got)):
            for i in range(vectors):
                if side or i:
                    total = total + weight_ref[side, i, shift] * ref[i]
        blocks[shift][...] = total


def unpack_kernel(share, parts, where_ref, *refs):
    blocks, (up, down, held) = refs[:parts], refs[parts:]
    place = where_ref[0]
    for shift in range(parts):
        held[lax.rem(place - shift + parts, parts)] = blocks[shift][...]
    for side, out in enumerate((up, down)):
        span = slice(side * share, (side + 1) * share)
        out[0, 0] = jnp.concatenate([held[q][:, span] for q in range(parts)], axis=1)


def vmem():
    return pl.BlockSpec(memory_space=pltpu.VMEM)


def smem():
    return pl.BlockSpec(memory_space=pltpu.SMEM)


def call(kernel, scalars, arrays, shapes, scratch=(), name=None, flops=0):
    moved = sum(a.size * 4 for a in arrays) + sum(math.prod(s) * 4 for s in shapes)
    return pl.pallas_call(
        kernel,
        out_shape=tuple(jax.ShapeDtypeStruct(s, f32) for s in shapes),
        in_specs=[smem()] * len(scalars) + [vmem()] * len(arrays),
        out_specs=tuple(vmem() for _ in shapes),
        scratch_shapes=[pltpu.VMEM(s, f32) for s in scratch],
        cost_estimate=pl.CostEstimate(flops=flops, bytes_accessed=moved, transcendentals=0),
        name=name,
    )(*scalars, *arrays)


def cas(rows, columns, count):
    angles = (rows * columns % count).astype(f32) * (2.0 * math.pi / count)
    return (jnp.cos(angles) + jnp.sin(angles)) / math.sqrt(count)


def exact(left_side, right_side):
    return jnp.einsum("kij,kjl->kil", left_side, right_side, precision=lax.Precision.HIGHEST)


def plain_inverse(coupling):
    identity = jnp.eye(coupling.shape[-1], dtype=f32)
    approx = identity + coupling

    def step(_, approx):
        return exact(approx, 2.0 * identity - exact(identity - coupling, approx))

    return lax.fori_loop(0, 6, step, approx)


def shards(drive, positions, materials, table, thickness, decay):
    parts = lax.axis_size("bloch")
    depth = lax.axis_size("stack")
    groups = depth // PAIR
    layers, m, columns = drive.shape[1], drive.shape[3], drive.shape[4]
    vectors = parts // PAIR
    share = columns // parts
    assert drive.shape[0] == 1 and depth % PAIR == 0 and parts % PAIR == 0 and columns % parts == 0
    place = lax.axis_index("bloch")
    stack_index = lax.axis_index("stack")
    group, parity = stack_index // PAIR, stack_index % PAIR
    place_ref, parity_ref = place[None].astype(jnp.int32), parity[None].astype(jnp.int32)
    partner = [(i, i ^ 1) for i in range(depth)]

    described = jnp.stack([materials.astype(f32), thickness])
    other = lax.ppermute(described, "stack", partner)
    both = jnp.where(parity == 0, jnp.concatenate([described, other], 1), jnp.concatenate([other, described], 1))
    kinds, thick = both[0].astype(jnp.int32), both[1]

    width = layers * 2 * share
    packed = call(
        functools.partial(pack_kernel, share, parts),
        [place_ref], [drive, positions[None, :]], [(m, width)] * parts, [(parts, m, width)], "pack",
    )

    def deal(blocks):
        out = [blocks[0]]
        for shift in range(1, parts):
            out.append(lax.ppermute(blocks[shift], "bloch", [(i, (i + shift) % parts) for i in range(parts)]))
        return out

    arrived = deal(packed)

    waves = jnp.arange(vectors, dtype=jnp.int32) * PAIR + parity
    factors = 1.0 + 0.5 * jnp.cos(waves.astype(f32) * (2.0 * math.pi / parts))
    first = (group == 0)[None].astype(jnp.int32)
    squares = [(vectors * PAIR, m, m)] * 3
    slab_d, slab_u, pair_d, pair_u, end_x, end_y, onward = call(
        functools.partial(matrices_kernel, layers, vectors),
        [factors, kinds, thick, first],
        [table, decay[None, :], decay[:, None]],
        [(vectors, PAIR, layers - 1, 2 * m, m)] * 2 + [(vectors, 4 * m, m)] * 4 + [(vectors, m, m)],
        squares, "matrices", 2 * 122 * m**3,
    )
    down_route = [(i, i + PAIR) for i in range(depth - PAIR)]
    up_route = [(i + PAIR, i) for i in range(depth - PAIR)]
    if groups == 2:
        prefix = suffix = lax.ppermute(onward, "stack", down_route + up_route)
        flags = jnp.stack([group == 1, group == 0]).astype(f32)
    else:
        flags = jnp.ones((2,), f32)
        top_t, down_t = end_x[:, 0:m], end_x[:, 3 * m:]
        up_t, end_t = end_y[:, 0:m], end_y[:, 3 * m:]

        def matrix_turn(turn, carry):
            prefix, suffix, falling, rising = carry
            prefix = jnp.where(group == turn, lax.ppermute(falling, "stack", down_route), prefix)
            suffix = jnp.where(group == groups - 1 - turn, lax.ppermute(rising, "stack", up_route), suffix)
            carry_d = exact(down_t, plain_inverse(exact(prefix, top_t)))
            carry_u = exact(up_t, plain_inverse(exact(suffix, end_t)))
            falling = jnp.where(group == turn, end_t + exact(carry_d, exact(prefix, up_t)), falling)
            rising = jnp.where(group == groups - 1 - turn, top_t + exact(carry_u, exact(suffix, down_t)), rising)
            return prefix, suffix, falling, rising

        nothing = jnp.zeros_like(onward)
        prefix, suffix, _, _ = lax.fori_loop(1, groups, matrix_turn, (nothing, nothing, end_t, top_t))
    from_d, from_u, own_d, own_u = call(
        functools.partial(boundary_kernel, vectors),
        [flags], [end_x, end_y, prefix, suffix], [(vectors, 4 * m, m)] * 4, squares, "boundary", 2 * 88 * m**3,
    )

    shifts = jnp.arange(parts, dtype=jnp.int32)
    wave_table = jnp.stack([waves, waves + 1 - 2 * parity])
    cells_from = (place - shifts) % parts
    kept, sent = call(
        functools.partial(transform_kernel, parts),
        [cas(wave_table[:, :, None], cells_from[None, None, :], parts)], arrived, [(vectors, m, width)] * 2, (), "transform",
    )
    got = lax.ppermute(sent, "stack", partner)
    inner, ends = call(
        functools.partial(sources_kernel, layers, share, vectors),
        [parity_ref], [kept, got, slab_d, slab_u, pair_d, pair_u],
        [(vectors, 4 * m, share), (vectors, 2, m, share)], [(PAIR, vectors, m, width)], "sources",
    )
    if groups == 2:
        chosen = jnp.where(group == 0, ends[:, 0], ends[:, 1])
        chosen = jnp.transpose(chosen, (1, 0, 2)).reshape(m, vectors * share)
        chosen = lax.ppermute(chosen, "stack", down_route + up_route)
        above = below = jnp.transpose(chosen.reshape(m, vectors, share), (1, 0, 2))
    else:
        end_s, top_s = ends[:, 0], ends[:, 1]
        carry_d = exact(down_t, plain_inverse(exact(prefix, top_t)))
        carry_u = exact(up_t, plain_inverse(exact(suffix, end_t)))

        def source_turn(turn, carry):
            above, below, falling, rising = carry
            above = jnp.where(group == turn, lax.ppermute(falling, "stack", down_route), above)
            below = jnp.where(group == groups - 1 - turn, lax.ppermute(rising, "stack", up_route), below)
            falling = jnp.where(group == turn, end_s + exact(carry_d, above + exact(prefix, top_s)), falling)
            rising = jnp.where(group == groups - 1 - turn, top_s + exact(carry_u, below + exact(suffix, end_s)), rising)
            return above, below, falling, rising

        nothing = jnp.zeros_like(end_s)
        above, below, _, _ = lax.fori_loop(1, groups, source_turn, (nothing, nothing, end_s, top_s))
    (answered,) = call(
        functools.partial(own_kernel, vectors),
        [], [inner, ends, own_d, own_u], [(vectors, 4 * m, share)], (), "own",
    )
    kept, sent = call(
        functools.partial(fields_kernel, vectors),
        [flags, parity_ref], [answered, above, below, from_d, from_u],
        [(vectors, m, 2 * share)] * 2, [(PAIR, vectors, m, 2 * share)], "fields",
    )
    got = lax.ppermute(sent, "stack", partner)

    cells_to = (place + shifts) % parts
    blocks = call(
        functools.partial(return_kernel, parts),
        [cas(wave_table[:, :, None], cells_to[None, None, :], parts)], [kept, got], [(m, 2 * share)] * parts, (), "return",
    )
    blocks = deal(blocks)
    return call(
        functools.partial(unpack_kernel, share, parts),
        [place_ref], blocks, [(1, 1, m, columns)] * 2, [(parts, m, 2 * share)], "unpack",
    )


def solution(mesh):
    in_specs = (
        P(("groups", "bloch"), "stack", None, None, None),
        P("groups"),
        P(("groups", "stack")),
        P(),
        P(("groups", "stack")),
        P(),
    )
    out_specs = (
        P(("groups", "bloch"), "stack", None, None),
        P(("groups", "bloch"), "stack", None, None),
    )
    return jax.shard_map(shards, mesh=mesh, in_specs=in_specs, out_specs=out_specs, check_vma=False)
```

```python
import functools
import math

import jax
import jax.numpy as jnp
import numpy as np
from jax import lax
from jax.experimental import pallas as pl
from jax.experimental.pallas import tpu as pltpu
from jax.sharding import PartitionSpec as P

PAIR = 2
NEGLIGIBLE = 4e-6

f32 = jnp.float32


def dot(left_side, right_side, precision=lax.Precision.HIGH):
    return lax.dot_general(
        left_side,
        right_side,
        (((1,), (0,)), ((), ())),
        precision=precision,
        preferred_element_type=f32,
    )


def eye(size):
    rows = lax.broadcasted_iota(jnp.int32, (size, size), 0)
    columns = lax.broadcasted_iota(jnp.int32, (size, size), 1)
    return (rows == columns).astype(f32)


def inverses(couplings, doublings, sum_ref, power_ref, coupling_ref):
    size = couplings[0].shape[0]
    count = len(couplings)
    identity = eye(size)
    sums = [identity + c for c in couplings]
    powers = [dot(c, c) for c in couplings]
    for turn in range(doublings):
        sums = [s + dot(s, p) for s, p in zip(sums, powers)]
        if turn < doublings - 1:
            powers = [dot(p, p) for p in powers]
    largest = functools.reduce(jnp.maximum, [jnp.sum(p * p, axis=0, keepdims=True) for p in powers])
    for i, (s, p, c) in enumerate(zip(sums, powers, couplings)):
        sum_ref[i] = s
        power_ref[i] = p
        coupling_ref[i] = c

    @pl.when(jnp.logical_not(jnp.sum(largest) <= NEGLIGIBLE))
    def _():
        exact = lax.Precision.HIGHEST

        def one(i, carry):
            def going(state):
                step, left_over = state
                return (step < 16) & (left_over > NEGLIGIBLE) & (left_over < 1e12)

            def double(state):
                step, _ = state
                power = dot(power_ref[i], power_ref[i], exact)
                power_ref[i] = power
                sum_ref[i] = sum_ref[i] + dot(sum_ref[i], power, exact)
                return (step + 1, jnp.sum(power * power))

            start = power_ref[i]
            _, left_over = lax.while_loop(going, double, (jnp.int32(0), jnp.sum(start * start)))

            @pl.when(jnp.logical_not(left_over <= NEGLIGIBLE))
            def _():
                system = eye(size) - coupling_ref[i]
                flipped = lax.dot_general(
                    system,
                    eye(size),
                    (((0,), (0,)), ((), ())),
                    precision=exact,
                    preferred_element_type=f32,
                )
                row_bound = jnp.max(jnp.sum(jnp.abs(system), axis=1, keepdims=True))
                column_bound = jnp.max(jnp.sum(jnp.abs(system), axis=0, keepdims=True))
                sum_ref[i] = flipped / (row_bound * column_bound)

                def refining(state):
                    step, gap = state
                    return (step < 100) & (gap > 1e-4)

                def refine(state):
                    step, _ = state
                    error = eye(size) - dot(eye(size) - coupling_ref[i], sum_ref[i], exact)
                    sum_ref[i] = sum_ref[i] + dot(sum_ref[i], error, exact)
                    return (step + 1, jnp.max(jnp.abs(error)))

                lax.while_loop(refining, refine, (jnp.int32(0), f32(1.0)))

            return carry

        lax.fori_loop(0, count, one, 0)

    return [sum_ref[i] for i in range(count)]


def inner_maps(above, below, gap):
    _, _, up_a, bottom_a = above
    top_b, down_b, _, _ = below
    identity = eye(gap.shape[0])
    mid_y_d = dot(top_b, gap)
    mid_x_u = dot(gap, bottom_a)
    mid_y_u = identity + dot(top_b, mid_x_u)
    return (
        (dot(up_a, mid_y_d), gap, mid_y_d, dot(down_b, gap)),
        (dot(up_a, mid_y_u), mid_x_u, mid_y_u, dot(down_b, mid_x_u)),
    )


def in_batches(count, work):
    size = 2 if count % 2 == 0 else 1
    if count == size:
        work(0, size)
    else:
        def step(i, carry):
            work(i * size, size)
            return carry

        lax.fori_loop(0, count // size, step, 0)


def segment(factor, thick, kind, table_ref, decay_ref):
    m = table_ref.shape[-1]
    row = jnp.exp(-(thick * factor) * decay_ref[...])
    column = jnp.sum(eye(m) * row, axis=1, keepdims=True)
    return tuple(column * table_ref[kind, b] * row for b in range(4))


def matrices_kernel(layers, vectors, edge, *refs):
    in_batches(vectors, lambda start, size: matrices_of(layers, start, size, edge, *refs))


def matrices_of(layers, start, size, edge, ids_ref, factor_ref, kind_ref, thick_ref, other_ref, table_ref, decay_ref, *refs):
    slab_d, slab_u, pair_d, pair_u, *ends, sum_ref, power_ref, coupling_ref = refs
    m = table_ref.shape[-1]
    parity, group = ids_ref[1], ids_ref[2]
    keys = [(k, j) for k in range(size) for j in range(PAIR)]
    segments = {}
    for k, j in keys:
        factor = factor_ref[(start + k) * PAIR + parity]
        for i in range(layers):
            kind = jnp.where(parity == j, kind_ref[i], other_ref[0, i].astype(jnp.int32))
            thick = jnp.where(parity == j, thick_ref[i], other_ref[1, i])
            segments[k, j, i] = segment(factor, thick, kind, table_ref, decay_ref)
    slabs = {(k, j): segments[k, j, 0] for k, j in keys}
    for i in range(1, layers):
        couplings = [dot(slabs[k, j][3], segments[k, j, i][0]) for k, j in keys]
        gaps = inverses(couplings, 2, sum_ref, power_ref, coupling_ref)
        for (k, j), gap in zip(keys, gaps):
            above, below = slabs[k, j], segments[k, j, i]
            by_d, by_u = inner_maps(above, below, gap)
            slab_d[start + k, j, i - 1, 0:m] = by_d[0]
            slab_d[start + k, j, i - 1, m:] = by_d[3]
            slab_u[start + k, j, i - 1, 0:m] = by_u[0]
            slab_u[start + k, j, i - 1, m:] = by_u[3]
            slabs[k, j] = (
                above[0] + dot(by_d[0], above[1]),
                dot(by_d[3], above[1]),
                dot(by_u[0], below[2]),
                below[3] + dot(by_u[3], below[2]),
            )
    couplings = [dot(slabs[k, 0][3], slabs[k, 1][0]) for k in range(size)]
    gaps = inverses(couplings, 2, sum_ref, power_ref, coupling_ref)
    for k, gap in enumerate(gaps):
        above, below = slabs[k, 0], slabs[k, 1]
        by_d, by_u = inner_maps(above, below, gap)
        k = start + k
        for r in range(4):
            pair_d[k, r * m:(r + 1) * m] = by_d[r]
            pair_u[k, r * m:(r + 1) * m] = by_u[r]
        if edge:
            answer, onward = ends
            top = group == 0
            inward = jnp.where(top, below[2], above[1])
            rows = [dot(jnp.where(top, u, d), inward) for d, u in zip(by_d, by_u)]
            rows[0] = rows[0] + jnp.where(top, 0.0, above[0])
            rows[3] = rows[3] + jnp.where(top, below[3], 0.0)
            for r in range(4):
                answer[k, r * m:(r + 1) * m] = rows[r]
            onward[k] = jnp.where(top, rows[3], rows[0])
        else:
            end_x, end_y = ends
            for r in range(4):
                from_x, from_y = dot(by_d[r], above[1]), dot(by_u[r], below[2])
                end_x[k, r * m:(r + 1) * m] = from_x + above[0] if r == 0 else from_x
                end_y[k, r * m:(r + 1) * m] = from_y + below[3] if r == 3 else from_y


def pack_kernel(share, parts, ids_ref, kind_ref, thick_ref, drive_ref, position_ref, *outs):
    *blocks, described, held = outs
    cell = ids_ref[0]
    offset = jnp.abs(cell - position_ref[...])
    offset = jnp.minimum(offset, parts - offset)
    envelope = 1.0 / (1.0 + offset.astype(f32))
    layers = drive_ref.shape[1]
    for i in range(layers):
        described[0, i] = kind_ref[i].astype(f32)
        described[1, i] = thick_ref[i]
    for q in range(parts):
        span = slice(q * share, (q + 1) * share)
        held[q] = jnp.concatenate(
            [drive_ref[0, i, d, :, span] * envelope[:, span] for i in range(layers) for d in range(2)], axis=1
        )
    for shift in range(parts):
        blocks[shift][...] = held[lax.rem(cell + shift, parts)]


def transform_kernel(parts, ids_ref, cas_ref, *refs):
    blocks, (_, kept, sent) = refs[:parts], refs[parts:]
    place, parity = ids_ref[0], ids_ref[1]
    loaded = [b[...] for b in blocks]
    cells = [lax.rem(place - shift + parts, parts) for shift in range(parts)]
    for side, out in ((parity, kept), (1 - parity, sent)):
        for i in range(out.shape[0]):
            wave = PAIR * i + side
            total = cas_ref[wave, cells[0]] * loaded[0]
            for shift in range(1, parts):
                total = total + cas_ref[wave, cells[shift]] * loaded[shift]
            out[i] = total


def sources_kernel(layers, share, vectors, edge, ids_ref, kept, got, slab_d, slab_u, pair_d, pair_u, slabs, *refs):
    m = kept.shape[1]
    parity, group = ids_ref[1], ids_ref[2]
    held = refs[-1]
    for k in range(vectors):
        held[parity, k] = kept[k]
        held[1 - parity, k] = got[k]
    ends = []
    for k in range(vectors):
        pair = []
        for j in range(PAIR):
            block = held[j, k]
            up, down = block[:, 0:share], block[:, share:2 * share]
            for i in range(1, layers):
                at = 2 * i * share
                up_b, down_b = block[:, at:at + share], block[:, at + share:at + 2 * share]
                both = dot(slab_d[k, j, i - 1], down) + dot(slab_u[k, j, i - 1], up_b)
                up, down = up + both[0:m], down_b + both[m:]
            slabs[k, 2 * j] = up
            slabs[k, 2 * j + 1] = down
            pair.append((up, down))
        if edge:
            rows = pl.ds(pl.multiple_of(jnp.where(group == 0, 3 * m, 0), 8), m)
            own = jnp.where(group == 0, pair[1][1], pair[0][0])
            ends.append(own + dot(pair_d[k, rows], pair[0][1]) + dot(pair_u[k, rows], pair[1][0]))
    if edge:
        refs[0][...] = jnp.concatenate(ends, axis=1)


def inner_kernel(vectors, slabs, pair_d, pair_u, inner):
    m = pair_d.shape[-1]
    for k in range(vectors):
        rows = dot(pair_d[k], slabs[k, 1]) + dot(pair_u[k], slabs[k, 2])
        inner[k, 0:m] = rows[0:m] + slabs[k, 0]
        inner[k, m:3 * m] = rows[m:3 * m]
        inner[k, 3 * m:] = rows[3 * m:] + slabs[k, 3]


def boundary_kernel(vectors, slabs, end, pair_d, pair_u, onward, arrived, inner, gap, bounced, sum_ref, power_ref, coupling_ref):
    share = slabs.shape[-1]
    inner_kernel(vectors, slabs, pair_d, pair_u, inner)
    bounced[...] = jnp.concatenate(
        [dot(arrived[k], end[:, k * share:(k + 1) * share]) for k in range(vectors)], axis=1
    )
    gaps = inverses([dot(arrived[k], onward[k]) for k in range(vectors)], 3, sum_ref, power_ref, coupling_ref)
    for k in range(vectors):
        gap[k] = gaps[k]


def fields_kernel(vectors, ids_ref, inner, answer, gap, bounced, crossed, kept, sent, held):
    m = inner.shape[1] // 4
    share = inner.shape[2]
    parity = ids_ref[1]
    inward = bounced[...] + crossed[...]
    for k in range(vectors):
        rows = inner[k] + dot(answer[k], dot(gap[k], inward[:, k * share:(k + 1) * share]))
        for j in range(PAIR):
            held[j, k] = jnp.concatenate([rows[2 * j * m:(2 * j + 1) * m], rows[(2 * j + 1) * m:(2 * j + 2) * m]], axis=1)
    for k in range(vectors):
        kept[k] = held[parity, k]
        sent[k] = held[1 - parity, k]


def return_kernel(parts, ids_ref, cas_ref, kept, got, *blocks):
    place, parity = ids_ref[0], ids_ref[1]
    vectors = kept.shape[0]
    mine, theirs = [kept[i] for i in range(vectors)], [got[i] for i in range(vectors)]
    for shift in range(parts):
        cell = lax.rem(place + shift, parts)
        total = None
        for side, fields in ((parity, mine), (1 - parity, theirs)):
            for i in range(vectors):
                term = cas_ref[cell, PAIR * i + side] * fields[i]
                total = term if total is None else total + term
        blocks[shift][...] = total


def unpack_kernel(share, parts, ids_ref, *refs):
    blocks, (up, down, held) = refs[:parts], refs[parts:]
    place = ids_ref[0]
    for shift in range(parts):
        held[lax.rem(place - shift + parts, parts)] = blocks[shift][...]
    for side, out in enumerate((up, down)):
        span = slice(side * share, (side + 1) * share)
        out[0, 0] = jnp.concatenate([held[q][:, span] for q in range(parts)], axis=1)


def vmem():
    return pl.BlockSpec(memory_space=pltpu.VMEM)


def smem():
    return pl.BlockSpec(memory_space=pltpu.SMEM)


def call(kernel, scalars, arrays, shapes, scratch=(), name=None, flops=0, limit=12, after=(), small=()):
    moved = sum(a.size * 4 for a in arrays) + sum(math.prod(s) * 4 for s in shapes)
    return pl.pallas_call(
        kernel,
        out_shape=tuple(jax.ShapeDtypeStruct(s, f32) for s in (*shapes, *small)),
        in_specs=[smem()] * len(scalars) + [vmem()] * len(arrays) + [pl.BlockSpec(memory_space=pl.ANY)] * len(after),
        out_specs=tuple([vmem()] * len(shapes) + [smem()] * len(small)),
        scratch_shapes=[pltpu.VMEM(s, f32) for s in scratch],
        cost_estimate=pl.CostEstimate(flops=flops, bytes_accessed=moved, transcendentals=0),
        compiler_params=pltpu.CompilerParams(vmem_limit_bytes=limit << 20),
        name=name,
    )(*scalars, *arrays, *after)


def exact(left_side, right_side):
    return jnp.einsum("kij,kjl->kil", left_side, right_side, precision=lax.Precision.HIGHEST)


def plain_inverse(coupling):
    identity = jnp.eye(coupling.shape[-1], dtype=f32)

    def step(_, approx):
        return exact(approx, 2.0 * identity - exact(identity - coupling, approx))

    return lax.fori_loop(0, 6, step, identity + coupling)


def chain(groups, group, depth, end_x, end_y, slabs, inner):
    m = end_x.shape[-1]
    down_route = [(i, i + PAIR) for i in range(depth - PAIR)]
    up_route = [(i + PAIR, i) for i in range(depth - PAIR)]
    top_t, down_t = end_x[:, 0:m], end_x[:, 3 * m:]
    up_t, end_t = end_y[:, 0:m], end_y[:, 3 * m:]
    top_s, end_s = inner[:, 0:m], inner[:, 3 * m:]

    def turn_of(turn, carry):
        prefix, suffix, falling, rising = carry
        from_above = [lax.ppermute(f, "stack", down_route) for f in falling]
        from_below = [lax.ppermute(r, "stack", up_route) for r in rising]
        prefix = [jnp.where(group == turn, new, old) for new, old in zip(from_above, prefix)]
        suffix = [jnp.where(group == groups - 1 - turn, new, old) for new, old in zip(from_below, suffix)]
        carry_d = exact(down_t, plain_inverse(exact(prefix[0], top_t)))
        carry_u = exact(up_t, plain_inverse(exact(suffix[0], end_t)))
        grown_d = [end_t + exact(carry_d, exact(prefix[0], up_t)), end_s + exact(carry_d, prefix[1] + exact(prefix[0], top_s))]
        grown_u = [top_t + exact(carry_u, exact(suffix[0], down_t)), top_s + exact(carry_u, suffix[1] + exact(suffix[0], end_s))]
        falling = [jnp.where(group == turn, new, old) for new, old in zip(grown_d, falling)]
        rising = [jnp.where(group == groups - 1 - turn, new, old) for new, old in zip(grown_u, rising)]
        return prefix, suffix, falling, rising

    nothing = [jnp.zeros_like(end_t), jnp.zeros_like(end_s)]
    prefix, suffix, _, _ = lax.fori_loop(1, groups, turn_of, (nothing, nothing, [end_t, end_s], [top_t, top_s]))
    lower = plain_inverse(exact(suffix[0], end_t))
    below = suffix[1] + exact(suffix[0], end_s)
    top_all = top_t + exact(up_t, exact(lower, exact(suffix[0], down_t)))
    source_all = top_s + exact(up_t, exact(lower, below))
    in_x = exact(plain_inverse(exact(prefix[0], top_all)), prefix[1] + exact(prefix[0], source_all))
    in_y = exact(lower, below + exact(suffix[0], exact(down_t, in_x)))
    return inner + exact(end_x, in_x) + exact(end_y, in_y)


def shards(drive, positions, materials, table, thickness, decay):
    parts = lax.axis_size("bloch")
    depth = lax.axis_size("stack")
    groups = depth // PAIR
    edge = groups == 2
    layers, m, columns = drive.shape[1], drive.shape[3], drive.shape[4]
    vectors = parts // PAIR
    share = columns // parts
    width = layers * 2 * share
    assert drive.shape[0] == 1 and depth % PAIR == 0 and parts % PAIR == 0 and columns % parts == 0
    stack_index = lax.axis_index("stack")
    group, parity = stack_index // PAIR, stack_index % PAIR
    ids = jnp.stack([lax.axis_index("bloch"), parity, group]).astype(jnp.int32)
    partner = [(i, i ^ 1) for i in range(depth)]
    across = [(i, i + PAIR) for i in range(depth - PAIR)] + [(i + PAIR, i) for i in range(depth - PAIR)]
    counts = np.arange(parts)
    angles = np.outer(counts, counts) % parts * (2.0 * math.pi / parts)
    cas = jnp.asarray((np.cos(angles) + np.sin(angles)) / math.sqrt(parts), f32)
    factors = jnp.asarray(1.0 + 0.5 * np.cos(counts * (2.0 * math.pi / parts)), f32)

    def deal(blocks):
        out = [blocks[0]]
        for shift in range(1, parts):
            out.append(lax.ppermute(blocks[shift], "bloch", [(i, (i + shift) % parts) for i in range(parts)]))
        return out

    *packed, described = call(
        functools.partial(pack_kernel, share, parts),
        [ids, materials, thickness], [drive, positions[None, :]],
        [(m, width)] * parts, [(parts, m, width)], "pack", small=[(2, layers)],
    )
    other = lax.ppermute(described, "stack", partner)
    arrived = deal(packed)

    squares = [(vectors * PAIR, m, m)] * 3
    end_shapes = [(vectors, 4 * m, m), (vectors, m, m)] if edge else [(vectors, 4 * m, m)] * 2
    slab_d, slab_u, pair_d, pair_u, *ends = call(
        functools.partial(matrices_kernel, layers, vectors, edge),
        [ids, factors, materials, thickness, other],
        [table, decay[None, :]],
        [(vectors, PAIR, layers - 1, 2 * m, m)] * 2 + [(vectors, 4 * m, m)] * 2 + end_shapes,
        squares, "matrices", 3000 * m**3, 32,
    )
    if edge:
        opposite = lax.ppermute(ends[1], "stack", across)

    kept, sent = call(
        functools.partial(transform_kernel, parts),
        [ids, cas], arrived, [(vectors, m, width)] * 2, (), "transform", after=[slab_d],
    )
    got = lax.ppermute(sent, "stack", partner)
    slabs, *end = call(
        functools.partial(sources_kernel, layers, share, vectors, edge),
        [ids], [kept, got, slab_d, slab_u, pair_d, pair_u],
        [(vectors, 4, m, share)] + ([(m, vectors * share)] if edge else []),
        [(PAIR, vectors, m, width)], "sources",
    )
    if edge:
        crossed = lax.ppermute(end[0], "stack", across)
        inner, gap, bounced = call(
            functools.partial(boundary_kernel, vectors),
            [], [slabs, end[0], pair_d, pair_u, ends[1], opposite],
            [(vectors, 4 * m, share), (vectors, m, m), (m, vectors * share)], squares, "boundary", 1000 * m**3,
        )
        kept, sent = call(
            functools.partial(fields_kernel, vectors),
            [ids], [inner, ends[0], gap, bounced, crossed],
            [(vectors, m, 2 * share)] * 2, [(PAIR, vectors, m, 2 * share)], "fields",
        )
    else:
        (inner,) = call(
            functools.partial(inner_kernel, vectors), [], [slabs, pair_d, pair_u], [(vectors, 4 * m, share)], (), "inner",
        )
        rows = chain(groups, group, depth, ends[0], ends[1], slabs, inner)
        sides = [jnp.concatenate([rows[:, 2 * j * m:(2 * j + 1) * m], rows[:, (2 * j + 1) * m:(2 * j + 2) * m]], 2) for j in range(PAIR)]
        kept = jnp.where(parity == 0, sides[0], sides[1])
        sent = jnp.where(parity == 0, sides[1], sides[0])
    got = lax.ppermute(sent, "stack", partner)

    blocks = call(
        functools.partial(return_kernel, parts), [ids, cas], [kept, got], [(m, 2 * share)] * parts, (), "return",
    )
    blocks = deal(blocks)
    return call(
        functools.partial(unpack_kernel, share, parts),
        [ids], blocks, [(1, 1, m, columns)] * 2, [(parts, m, 2 * share)], "unpack",
    )


def solution(mesh):
    in_specs = (
        P(("groups", "bloch"), "stack", None, None, None),
        P("groups"),
        P(("groups", "stack")),
        P(),
        P(("groups", "stack")),
        P(),
    )
    out_specs = (
        P(("groups", "bloch"), "stack", None, None),
        P(("groups", "bloch"), "stack", None, None),
    )
    return jax.shard_map(shards, mesh=mesh, in_specs=in_specs, out_specs=out_specs, check_vma=False)
```

```python
import functools
import math

import jax
import jax.numpy as jnp
from jax import lax
from jax.experimental import pallas as pl
from jax.experimental.pallas import tpu as pltpu
from jax.sharding import PartitionSpec as P

PAIR = 2
NEGLIGIBLE = 4e-6

f32 = jnp.float32


def dot(left_side, right_side, precision=lax.Precision.HIGH):
    return lax.dot_general(
        left_side,
        right_side,
        (((1,), (0,)), ((), ())),
        precision=precision,
        preferred_element_type=f32,
    )


def eye(size):
    rows = lax.broadcasted_iota(jnp.int32, (size, size), 0)
    columns = lax.broadcasted_iota(jnp.int32, (size, size), 1)
    return (rows == columns).astype(f32)


def inverses(couplings, doublings, sum_ref, power_ref, coupling_ref):
    size = couplings[0].shape[0]
    count = len(couplings)
    identity = eye(size)
    sums = [identity + c for c in couplings]
    powers = [dot(c, c) for c in couplings]
    for turn in range(doublings):
        sums = [s + dot(s, p) for s, p in zip(sums, powers)]
        if turn < doublings - 1:
            powers = [dot(p, p) for p in powers]
    largest = functools.reduce(jnp.maximum, [jnp.sum(p * p, axis=0, keepdims=True) for p in powers])
    for i, (s, p, c) in enumerate(zip(sums, powers, couplings)):
        sum_ref[i] = s
        power_ref[i] = p
        coupling_ref[i] = c

    @pl.when(jnp.logical_not(jnp.sum(largest) <= NEGLIGIBLE))
    def _():
        exact = lax.Precision.HIGHEST

        def one(i, carry):
            def going(state):
                step, left_over = state
                return (step < 16) & (left_over > NEGLIGIBLE) & (left_over < 1e12)

            def double(state):
                step, _ = state
                power = dot(power_ref[i], power_ref[i], exact)
                power_ref[i] = power
                sum_ref[i] = sum_ref[i] + dot(sum_ref[i], power, exact)
                return (step + 1, jnp.sum(power * power))

            start = power_ref[i]
            _, left_over = lax.while_loop(going, double, (jnp.int32(0), jnp.sum(start * start)))

            @pl.when(jnp.logical_not(left_over <= NEGLIGIBLE))
            def _():
                system = eye(size) - coupling_ref[i]
                flipped = lax.dot_general(
                    system,
                    eye(size),
                    (((0,), (0,)), ((), ())),
                    precision=exact,
                    preferred_element_type=f32,
                )
                row_bound = jnp.max(jnp.sum(jnp.abs(system), axis=1, keepdims=True))
                column_bound = jnp.max(jnp.sum(jnp.abs(system), axis=0, keepdims=True))
                sum_ref[i] = flipped / (row_bound * column_bound)

                def refining(state):
                    step, gap = state
                    return (step < 100) & (gap > 1e-4)

                def refine(state):
                    step, _ = state
                    error = eye(size) - dot(eye(size) - coupling_ref[i], sum_ref[i], exact)
                    sum_ref[i] = sum_ref[i] + dot(sum_ref[i], error, exact)
                    return (step + 1, jnp.max(jnp.abs(error)))

                lax.while_loop(refining, refine, (jnp.int32(0), f32(1.0)))

            return carry

        lax.fori_loop(0, count, one, 0)

    return [sum_ref[i] for i in range(count)]


def inner_maps(above, below, gap):
    _, _, up_a, bottom_a = above
    top_b, down_b, _, _ = below
    identity = eye(gap.shape[0])
    mid_y_d = dot(top_b, gap)
    mid_x_u = dot(gap, bottom_a)
    mid_y_u = identity + dot(top_b, mid_x_u)
    return (
        (dot(up_a, mid_y_d), gap, mid_y_d, dot(down_b, gap)),
        (dot(up_a, mid_y_u), mid_x_u, mid_y_u, dot(down_b, mid_x_u)),
    )


def in_batches(count, work):
    size = 2 if count % 2 == 0 else 1
    if count == size:
        work(0, size)
    else:
        def step(i, carry):
            work(i * size, size)
            return carry

        lax.fori_loop(0, count // size, step, 0)


def pick(values, index):
    value = f32(values[0])
    for i in range(1, len(values)):
        value = jnp.where(index == i, f32(values[i]), value)
    return value


def cas(row, column, count):
    angles = [2.0 * math.pi * i / count for i in range(count)]
    return pick([(math.cos(a) + math.sin(a)) / math.sqrt(count) for a in angles], lax.rem(row * column, count))


def segment(factor, thick, blocks, decay):
    m = decay.shape[-1]
    row = jnp.exp(-(thick * factor) * decay)
    column = jnp.sum(eye(m) * row, axis=1, keepdims=True)
    return tuple(column * blocks[b] * row for b in range(4))


def slabs_kernel(layers, vectors, parts, edge, ids_ref, other_ref, kind_hbm, thick_hbm, table_hbm, decay_hbm, *refs):
    *outs, sum_ref, power_ref, coupling_ref, kind_ref, thick_ref, blocks_ref, decay_ref, sems, block_sems = refs
    parity = ids_ref[1]
    small = [
        pltpu.make_async_copy(kind_hbm, kind_ref, sems.at[0]),
        pltpu.make_async_copy(thick_hbm, thick_ref, sems.at[1]),
        pltpu.make_async_copy(decay_hbm, decay_ref, sems.at[2]),
    ]
    for copy in small:
        copy.start()
    small[0].wait()
    large = {}
    for i in range(layers):
        for j in range(PAIR):
            kind = jnp.where(parity == j, kind_ref[i], other_ref[0, i].astype(jnp.int32))
            large[j, i] = pltpu.make_async_copy(table_hbm.at[kind], blocks_ref.at[j, i], block_sems.at[j, i])
            large[j, i].start()
    for copy in small[1:]:
        copy.wait()
    for i in range(layers):
        for j in range(PAIR):
            large[j, i].wait()
    scratch = sum_ref, power_ref, coupling_ref
    in_batches(vectors, lambda start, size: slabs_of(
        layers, parts, start, size, edge, ids_ref, other_ref, thick_ref, blocks_ref, decay_ref, outs, scratch))


def slabs_of(layers, parts, start, size, edge, ids_ref, other_ref, thick_ref, blocks_ref, decay_ref, outs, scratch):
    slab_d, slab_u, slab_ref, gap_ref, *onward = outs
    m = decay_ref.shape[-1]
    parity, top = ids_ref[1], ids_ref[2] == 0
    keys = [(k, j) for k in range(size) for j in range(PAIR)]
    factors = [1.0 + 0.5 * math.cos(2.0 * math.pi * i / parts) for i in range(parts)]
    segments = {}
    for k, j in keys:
        factor = pick(factors, (start + k) * PAIR + parity)
        for i in range(layers):
            thick = jnp.where(parity == j, thick_ref[i], other_ref[1, i])
            segments[k, j, i] = segment(factor, thick, [blocks_ref[j, i, b] for b in range(4)], decay_ref[...])
    slabs = {(k, j): segments[k, j, 0] for k, j in keys}
    for i in range(1, layers):
        couplings = [dot(slabs[k, j][3], segments[k, j, i][0]) for k, j in keys]
        gaps = inverses(couplings, 2, *scratch)
        for (k, j), gap in zip(keys, gaps):
            above, below = slabs[k, j], segments[k, j, i]
            by_d, by_u = inner_maps(above, below, gap)
            slab_d[start + k, j, i - 1, 0:m] = by_d[0]
            slab_d[start + k, j, i - 1, m:] = by_d[3]
            slab_u[start + k, j, i - 1, 0:m] = by_u[0]
            slab_u[start + k, j, i - 1, m:] = by_u[3]
            slabs[k, j] = (
                above[0] + dot(by_d[0], above[1]),
                dot(by_d[3], above[1]),
                dot(by_u[0], below[2]),
                below[3] + dot(by_u[3], below[2]),
            )
    for k, j in keys:
        for b in range(4):
            slab_ref[start + k, j, b] = slabs[k, j][b]
    couplings = [dot(slab_ref[start + k, 0, 3], slab_ref[start + k, 1, 0]) for k in range(size)]
    gaps = inverses(couplings, 2, *scratch)
    for k, gap in enumerate(gaps):
        gap_ref[start + k] = gap
        above, below = [[slab_ref[start + k, j, b] for b in range(4)] for j in range(PAIR)]
        if edge:
            first = dot(jnp.where(top, above[3], above[2]), jnp.where(top, below[2], below[0]))
            left = jnp.where(top, below[1], first)
            right = jnp.where(top, first, above[1])
            onward[0][start + k] = jnp.where(top, below[3], above[0]) + dot(left, dot(gap, right))


def maps_kernel(vectors, edge, ids_ref, slab_ref, gap_ref, *refs):
    pair_d, pair_u, *ends = refs[1:] if edge else refs
    m = gap_ref.shape[-1]
    top = ids_ref[2] == 0

    def maps_of(start, size):
        for k in range(size):
            k = start + k
            above = [slab_ref[k, 0, b] for b in range(4)]
            below = [slab_ref[k, 1, b] for b in range(4)]
            by_d, by_u = inner_maps(above, below, gap_ref[k])
            for r in range(4):
                pair_d[k, r * m:(r + 1) * m] = by_d[r]
                pair_u[k, r * m:(r + 1) * m] = by_u[r]
            if edge:
                inward = jnp.where(top, below[2], above[1])
                for r in range(4):
                    row = dot(jnp.where(top, by_u[r], by_d[r]), inward)
                    if r == 0:
                        row = row + jnp.where(top, 0.0, above[0])
                    if r == 3:
                        row = row + jnp.where(top, below[3], 0.0)
                    ends[0][k, r * m:(r + 1) * m] = row
            else:
                end_x, end_y = ends
                for r in range(4):
                    from_x, from_y = dot(by_d[r], above[1]), dot(by_u[r], below[2])
                    end_x[k, r * m:(r + 1) * m] = from_x + above[0] if r == 0 else from_x
                    end_y[k, r * m:(r + 1) * m] = from_y + below[3] if r == 3 else from_y

    in_batches(vectors, maps_of)


def pack_kernel(share, parts, ids_ref, drive_hbm, position_hbm, kind_hbm, thick_hbm, *outs):
    *blocks, described, held, drive_ref, position_ref, kind_ref, thick_ref, sems, drive_sems = outs
    layers = drive_hbm.shape[1]
    small = [
        pltpu.make_async_copy(position_hbm, position_ref, sems.at[0]),
        pltpu.make_async_copy(kind_hbm, kind_ref, sems.at[1]),
        pltpu.make_async_copy(thick_hbm, thick_ref, sems.at[2]),
    ]
    large = {
        (i, d): pltpu.make_async_copy(drive_hbm.at[0, i, d], drive_ref.at[i, d], drive_sems.at[i, d])
        for i in range(layers) for d in range(2)
    }
    for copy in [*small, *large.values()]:
        copy.start()
    for copy in small:
        copy.wait()
    cell = ids_ref[0]
    offset = jnp.abs(cell - position_ref[...])
    offset = jnp.minimum(offset, parts - offset)
    envelope = 1.0 / (1.0 + offset.astype(f32))
    for i in range(layers):
        described[0, i] = kind_ref[i].astype(f32)
        described[1, i] = thick_ref[i]
    for copy in large.values():
        copy.wait()
    for q in range(parts):
        span = slice(q * share, (q + 1) * share)
        held[q] = jnp.concatenate(
            [drive_ref[i, d, :, span] * envelope[:, span] for i in range(layers) for d in range(2)], axis=1
        )
    for step in range(parts):
        blocks[step][...] = held[cell ^ step]


def transform_kernel(parts, ids_ref, *refs):
    blocks, (_, kept, sent) = refs[:parts], refs[parts:]
    place, parity = ids_ref[0], ids_ref[1]
    loaded = [b[...] for b in blocks]
    cells = [place ^ step for step in range(parts)]
    for side, out in ((parity, kept), (1 - parity, sent)):
        for i in range(out.shape[0]):
            wave = PAIR * i + side
            total = cas(wave, cells[0], parts) * loaded[0]
            for step in range(1, parts):
                total = total + cas(wave, cells[step], parts) * loaded[step]
            out[i] = total


def sources_kernel(layers, share, vectors, edge, ids_ref, kept, got, slab_d, slab_u, pair_d, pair_u, slabs, *refs):
    m = kept.shape[1]
    parity, group = ids_ref[1], ids_ref[2]
    held = refs[-1]
    for k in range(vectors):
        held[parity, k] = kept[k]
        held[1 - parity, k] = got[k]
    ends = []
    for k in range(vectors):
        pair = []
        for j in range(PAIR):
            block = held[j, k]
            up, down = block[:, 0:share], block[:, share:2 * share]
            for i in range(1, layers):
                at = 2 * i * share
                up_b, down_b = block[:, at:at + share], block[:, at + share:at + 2 * share]
                both = dot(slab_d[k, j, i - 1], down) + dot(slab_u[k, j, i - 1], up_b)
                up, down = up + both[0:m], down_b + both[m:]
            slabs[k, 2 * j] = up
            slabs[k, 2 * j + 1] = down
            pair.append((up, down))
        if edge:
            rows = pl.ds(pl.multiple_of(jnp.where(group == 0, 3 * m, 0), 8), m)
            own = jnp.where(group == 0, pair[1][1], pair[0][0])
            ends.append(own + dot(pair_d[k, rows], pair[0][1]) + dot(pair_u[k, rows], pair[1][0]))
    if edge:
        refs[0][...] = jnp.concatenate(ends, axis=1)


def inner_kernel(vectors, slabs, pair_d, pair_u, inner):
    m = pair_d.shape[-1]
    for k in range(vectors):
        rows = dot(pair_d[k], slabs[k, 1]) + dot(pair_u[k], slabs[k, 2])
        inner[k, 0:m] = rows[0:m] + slabs[k, 0]
        inner[k, m:3 * m] = rows[m:3 * m]
        inner[k, 3 * m:] = rows[3 * m:] + slabs[k, 3]


def boundary_kernel(vectors, slabs, end, pair_d, pair_u, onward, arrived, inner, gap, bounced, sum_ref, power_ref, coupling_ref):
    share = slabs.shape[-1]
    inner_kernel(vectors, slabs, pair_d, pair_u, inner)
    bounced[...] = jnp.concatenate(
        [dot(arrived[k], end[:, k * share:(k + 1) * share]) for k in range(vectors)], axis=1
    )
    gaps = inverses([dot(arrived[k], onward[k]) for k in range(vectors)], 3, sum_ref, power_ref, coupling_ref)
    for k in range(vectors):
        gap[k] = gaps[k]


def fields_kernel(vectors, ids_ref, inner, answer, gap, bounced, crossed, kept, sent, held):
    m = inner.shape[1] // 4
    share = inner.shape[2]
    parity = ids_ref[1]
    inward = bounced[...] + crossed[...]
    for k in range(vectors):
        rows = inner[k] + dot(answer[k], dot(gap[k], inward[:, k * share:(k + 1) * share]))
        for j in range(PAIR):
            held[j, k] = jnp.concatenate([rows[2 * j * m:(2 * j + 1) * m], rows[(2 * j + 1) * m:(2 * j + 2) * m]], axis=1)
    for k in range(vectors):
        kept[k] = held[parity, k]
        sent[k] = held[1 - parity, k]


def return_kernel(parts, ids_ref, kept, got, *blocks):
    place, parity = ids_ref[0], ids_ref[1]
    vectors = kept.shape[0]
    mine, theirs = [kept[i] for i in range(vectors)], [got[i] for i in range(vectors)]
    for step in range(parts):
        cell = place ^ step
        total = None
        for side, fields in ((parity, mine), (1 - parity, theirs)):
            for i in range(vectors):
                term = cas(cell, PAIR * i + side, parts) * fields[i]
                total = term if total is None else total + term
        blocks[step][...] = total


def unpack_kernel(share, parts, ids_ref, *refs):
    blocks, (up, down, held) = refs[:parts], refs[parts:]
    place = ids_ref[0]
    for step in range(parts):
        held[place ^ step] = blocks[step][...]
    for side, out in enumerate((up, down)):
        span = slice(side * share, (side + 1) * share)
        out[0, 0] = jnp.concatenate([held[q][:, span] for q in range(parts)], axis=1)


def vmem():
    return pl.BlockSpec(memory_space=pltpu.VMEM)


def smem():
    return pl.BlockSpec(memory_space=pltpu.SMEM)


def call(kernel, scalars, arrays, shapes, scratch=(), name=None, flops=0, limit=12, after=(), small=(), far=()):
    moved = sum(a.size * 4 for a in (*arrays, *far)) + sum(math.prod(s) * 4 for s in shapes)
    return pl.pallas_call(
        kernel,
        out_shape=tuple(jax.ShapeDtypeStruct(s, f32) for s in (*shapes, *small)),
        in_specs=[smem()] * len(scalars)
        + [vmem()] * len(arrays)
        + [pl.BlockSpec(memory_space=pltpu.HBM)] * len(far)
        + [pl.BlockSpec(memory_space=pl.ANY)] * len(after),
        out_specs=tuple([vmem()] * len(shapes) + [smem()] * len(small)),
        scratch_shapes=[pltpu.VMEM(s, f32) if isinstance(s, tuple) else s for s in scratch],
        cost_estimate=pl.CostEstimate(flops=flops, bytes_accessed=moved, transcendentals=0),
        compiler_params=pltpu.CompilerParams(vmem_limit_bytes=limit << 20),
        name=name,
    )(*scalars, *arrays, *far, *after)


def exact(left_side, right_side):
    return jnp.einsum("kij,kjl->kil", left_side, right_side, precision=lax.Precision.HIGHEST)


def plain_inverse(coupling):
    identity = jnp.eye(coupling.shape[-1], dtype=f32)

    def step(_, approx):
        return exact(approx, 2.0 * identity - exact(identity - coupling, approx))

    return lax.fori_loop(0, 6, step, identity + coupling)


def chain(groups, group, depth, end_x, end_y, slabs, inner):
    m = end_x.shape[-1]
    down_route = [(i, i + PAIR) for i in range(depth - PAIR)]
    up_route = [(i + PAIR, i) for i in range(depth - PAIR)]
    top_t, down_t = end_x[:, 0:m], end_x[:, 3 * m:]
    up_t, end_t = end_y[:, 0:m], end_y[:, 3 * m:]
    top_s, end_s = inner[:, 0:m], inner[:, 3 * m:]

    def turn_of(turn, carry):
        prefix, suffix, falling, rising = carry
        from_above = [lax.ppermute(f, "stack", down_route) for f in falling]
        from_below = [lax.ppermute(r, "stack", up_route) for r in rising]
        prefix = [jnp.where(group == turn, new, old) for new, old in zip(from_above, prefix)]
        suffix = [jnp.where(group == groups - 1 - turn, new, old) for new, old in zip(from_below, suffix)]
        carry_d = exact(down_t, plain_inverse(exact(prefix[0], top_t)))
        carry_u = exact(up_t, plain_inverse(exact(suffix[0], end_t)))
        grown_d = [end_t + exact(carry_d, exact(prefix[0], up_t)), end_s + exact(carry_d, prefix[1] + exact(prefix[0], top_s))]
        grown_u = [top_t + exact(carry_u, exact(suffix[0], down_t)), top_s + exact(carry_u, suffix[1] + exact(suffix[0], end_s))]
        falling = [jnp.where(group == turn, new, old) for new, old in zip(grown_d, falling)]
        rising = [jnp.where(group == groups - 1 - turn, new, old) for new, old in zip(grown_u, rising)]
        return prefix, suffix, falling, rising

    nothing = [jnp.zeros_like(end_t), jnp.zeros_like(end_s)]
    prefix, suffix, _, _ = lax.fori_loop(1, groups, turn_of, (nothing, nothing, [end_t, end_s], [top_t, top_s]))
    lower = plain_inverse(exact(suffix[0], end_t))
    below = suffix[1] + exact(suffix[0], end_s)
    top_all = top_t + exact(up_t, exact(lower, exact(suffix[0], down_t)))
    source_all = top_s + exact(up_t, exact(lower, below))
    in_x = exact(plain_inverse(exact(prefix[0], top_all)), prefix[1] + exact(prefix[0], source_all))
    in_y = exact(lower, below + exact(suffix[0], exact(down_t, in_x)))
    return inner + exact(end_x, in_x) + exact(end_y, in_y)


def shards(drive, positions, materials, table, thickness, decay):
    parts = lax.axis_size("bloch")
    depth = lax.axis_size("stack")
    groups = depth // PAIR
    edge = groups == 2
    layers, m, columns = drive.shape[1], drive.shape[3], drive.shape[4]
    vectors = parts // PAIR
    share = columns // parts
    width = layers * 2 * share
    assert drive.shape[0] == 1 and depth % PAIR == 0 and columns % parts == 0
    assert parts % PAIR == 0 and parts & (parts - 1) == 0
    stack_index = lax.axis_index("stack")
    group, parity = stack_index // PAIR, stack_index % PAIR
    ids = jnp.stack([lax.axis_index("bloch"), parity, group]).astype(jnp.int32)
    partner = [(i, i ^ 1) for i in range(depth)]
    across = [(i, i + PAIR) for i in range(depth - PAIR)] + [(i + PAIR, i) for i in range(depth - PAIR)]
    dma = pltpu.SemaphoreType.DMA

    def deal(blocks):
        out = {0: blocks[0]}
        for step in sorted(range(1, parts), reverse=True):
            out[step] = lax.ppermute(blocks[step], "bloch", [(i, i ^ step) for i in range(parts)])
        return [out[step] for step in range(parts)]

    *packed, described = call(
        functools.partial(pack_kernel, share, parts),
        [ids], [], [(m, width)] * parts,
        [(parts, m, width), (layers, 2, m, columns), pltpu.VMEM((1, columns), jnp.int32), pltpu.SMEM((layers,), jnp.int32),
         pltpu.SMEM((layers,), f32), dma((3,)), dma((layers, 2))],
        "pack", small=[(2, layers)], far=[drive, positions[None, :], materials, thickness],
    )
    other = lax.ppermute(described, "stack", partner)
    arrived = deal(packed)

    squares = [(vectors * PAIR, m, m)] * 3
    slab_d, slab_u, slab, gap, *onward = call(
        functools.partial(slabs_kernel, layers, vectors, parts, edge),
        [ids, other], [],
        [(vectors, PAIR, layers - 1, 2 * m, m)] * 2 + [(vectors, PAIR, 4, m, m), (vectors, m, m)] + [(vectors, m, m)] * edge,
        squares + [pltpu.SMEM((layers,), jnp.int32), pltpu.SMEM((layers,), f32), (PAIR, layers, 4, m, m), (1, m),
                   dma((3,)), dma((PAIR, layers))],
        "slabs", 3000 * m**3, 32, far=[materials, thickness, table, decay[None, :]],
    )
    if edge:
        opposite = lax.ppermute(onward[0], "stack", across)
    pair_d, pair_u, *ends = call(
        functools.partial(maps_kernel, vectors, edge),
        [ids], [slab, gap], [(vectors, 4 * m, m)] * (3 if edge else 4), (), "maps", 500 * m**3, after=onward,
    )

    kept, sent = call(
        functools.partial(transform_kernel, parts),
        [ids], arrived, [(vectors, m, width)] * 2, (), "transform", after=[pair_d],
    )
    got = lax.ppermute(sent, "stack", partner)
    slabs, *end = call(
        functools.partial(sources_kernel, layers, share, vectors, edge),
        [ids], [kept, got, slab_d, slab_u, pair_d, pair_u],
        [(vectors, 4, m, share)] + ([(m, vectors * share)] if edge else []),
        [(PAIR, vectors, m, width)], "sources",
    )
    if edge:
        crossed = lax.ppermute(end[0], "stack", across)
        inner, gate, bounced = call(
            functools.partial(boundary_kernel, vectors),
            [], [slabs, end[0], pair_d, pair_u, onward[0], opposite],
            [(vectors, 4 * m, share), (vectors, m, m), (m, vectors * share)], squares, "boundary", 1000 * m**3,
        )
        kept, sent = call(
            functools.partial(fields_kernel, vectors),
            [ids], [inner, ends[0], gate, bounced, crossed],
            [(vectors, m, 2 * share)] * 2, [(PAIR, vectors, m, 2 * share)], "fields",
        )
    else:
        (inner,) = call(
            functools.partial(inner_kernel, vectors), [], [slabs, pair_d, pair_u], [(vectors, 4 * m, share)], (), "inner",
        )
        rows = chain(groups, group, depth, ends[0], ends[1], slabs, inner)
        sides = [jnp.concatenate([rows[:, 2 * j * m:(2 * j + 1) * m], rows[:, (2 * j + 1) * m:(2 * j + 2) * m]], 2) for j in range(PAIR)]
        kept = jnp.where(parity == 0, sides[0], sides[1])
        sent = jnp.where(parity == 0, sides[1], sides[0])
    got = lax.ppermute(sent, "stack", partner)

    blocks = call(
        functools.partial(return_kernel, parts), [ids], [kept, got], [(m, 2 * share)] * parts, (), "return",
    )
    blocks = deal(blocks)
    return call(
        functools.partial(unpack_kernel, share, parts),
        [ids], blocks, [(1, 1, m, columns)] * 2, [(parts, m, 2 * share)], "unpack",
    )


def solution(mesh):
    in_specs = (
        P(("groups", "bloch"), "stack", None, None, None),
        P("groups"),
        P(("groups", "stack")),
        P(),
        P(("groups", "stack")),
        P(),
    )
    out_specs = (
        P(("groups", "bloch"), "stack", None, None),
        P(("groups", "bloch"), "stack", None, None),
    )
    return jax.shard_map(shards, mesh=mesh, in_specs=in_specs, out_specs=out_specs, check_vma=False)
```

```python
import functools
import math

import jax
import jax.numpy as jnp
from jax import lax
from jax.experimental import pallas as pl
from jax.experimental.pallas import tpu as pltpu
from jax.sharding import PartitionSpec as P

PAIR = 2
NEGLIGIBLE = 4e-6

f32 = jnp.float32


def dot(left_side, right_side, precision=lax.Precision.HIGH):
    return lax.dot_general(
        left_side,
        right_side,
        (((1,), (0,)), ((), ())),
        precision=precision,
        preferred_element_type=f32,
    )


def eye(size):
    rows = lax.broadcasted_iota(jnp.int32, (size, size), 0)
    columns = lax.broadcasted_iota(jnp.int32, (size, size), 1)
    return (rows == columns).astype(f32)


def inverses(couplings, doublings, sum_ref, power_ref, coupling_ref):
    size = couplings[0].shape[0]
    count = len(couplings)
    identity = eye(size)
    sums = [identity + c for c in couplings]
    powers = [dot(c, c) for c in couplings]
    for turn in range(doublings):
        sums = [s + dot(s, p) for s, p in zip(sums, powers)]
        if turn < doublings - 1:
            powers = [dot(p, p) for p in powers]
    largest = functools.reduce(jnp.maximum, [jnp.sum(p * p, axis=0, keepdims=True) for p in powers])
    for i, (s, p, c) in enumerate(zip(sums, powers, couplings)):
        sum_ref[i] = s
        power_ref[i] = p
        coupling_ref[i] = c

    @pl.when(jnp.logical_not(jnp.sum(largest) <= NEGLIGIBLE))
    def _():
        exact = lax.Precision.HIGHEST

        def one(i, carry):
            def going(state):
                step, left_over = state
                return (step < 16) & (left_over > NEGLIGIBLE) & (left_over < 1e12)

            def double(state):
                step, _ = state
                power = dot(power_ref[i], power_ref[i], exact)
                power_ref[i] = power
                sum_ref[i] = sum_ref[i] + dot(sum_ref[i], power, exact)
                return (step + 1, jnp.sum(power * power))

            start = power_ref[i]
            _, left_over = lax.while_loop(going, double, (jnp.int32(0), jnp.sum(start * start)))

            @pl.when(jnp.logical_not(left_over <= NEGLIGIBLE))
            def _():
                system = eye(size) - coupling_ref[i]
                flipped = lax.dot_general(
                    system,
                    eye(size),
                    (((0,), (0,)), ((), ())),
                    precision=exact,
                    preferred_element_type=f32,
                )
                row_bound = jnp.max(jnp.sum(jnp.abs(system), axis=1, keepdims=True))
                column_bound = jnp.max(jnp.sum(jnp.abs(system), axis=0, keepdims=True))
                sum_ref[i] = flipped / (row_bound * column_bound)

                def refining(state):
                    step, gap = state
                    return (step < 100) & (gap > 1e-4)

                def refine(state):
                    step, _ = state
                    error = eye(size) - dot(eye(size) - coupling_ref[i], sum_ref[i], exact)
                    sum_ref[i] = sum_ref[i] + dot(sum_ref[i], error, exact)
                    return (step + 1, jnp.max(jnp.abs(error)))

                lax.while_loop(refining, refine, (jnp.int32(0), f32(1.0)))

            return carry

        lax.fori_loop(0, count, one, 0)

    return [sum_ref[i] for i in range(count)]


def inner_maps(above, below, gap):
    _, _, up_a, bottom_a = above
    top_b, down_b, _, _ = below
    identity = eye(gap.shape[0])
    mid_y_d = dot(top_b, gap)
    mid_x_u = dot(gap, bottom_a)
    mid_y_u = identity + dot(top_b, mid_x_u)
    return (
        (dot(up_a, mid_y_d), gap, mid_y_d, dot(down_b, gap)),
        (dot(up_a, mid_y_u), mid_x_u, mid_y_u, dot(down_b, mid_x_u)),
    )


def in_batches(count, work):
    size = 2 if count % 2 == 0 else 1
    if count == size:
        work(0, size)
    else:
        def step(i, carry):
            work(i * size, size)
            return carry

        lax.fori_loop(0, count // size, step, 0)


def pick(values, index):
    value = f32(values[0])
    for i in range(1, len(values)):
        value = jnp.where(index == i, f32(values[i]), value)
    return value


def cas(row, column, count):
    angles = [2.0 * math.pi * i / count for i in range(count)]
    return pick([(math.cos(a) + math.sin(a)) / math.sqrt(count) for a in angles], lax.rem(row * column, count))


def segment(factor, thick, blocks, decay):
    m = decay.shape[-1]
    row = jnp.exp(-(thick * factor) * decay)
    column = jnp.sum(eye(m) * row, axis=1, keepdims=True)
    return tuple(column * blocks[b] * row for b in range(4))


def slabs_kernel(layers, vectors, parts, edge, ids_ref, other_ref, kind_hbm, thick_hbm, table_hbm, decay_hbm, *refs):
    *outs, sum_ref, power_ref, coupling_ref, kind_ref, thick_ref, blocks_ref, decay_ref, sems, block_sems = refs
    parity = ids_ref[1]
    small = [
        pltpu.make_async_copy(kind_hbm, kind_ref, sems.at[0]),
        pltpu.make_async_copy(thick_hbm, thick_ref, sems.at[1]),
        pltpu.make_async_copy(decay_hbm, decay_ref, sems.at[2]),
    ]
    for copy in small:
        copy.start()
    small[0].wait()
    large = {}
    for i in range(layers):
        for j in range(PAIR):
            kind = jnp.where(parity == j, kind_ref[i], other_ref[0, i].astype(jnp.int32))
            large[j, i] = pltpu.make_async_copy(table_hbm.at[kind], blocks_ref.at[j, i], block_sems.at[j, i])
            large[j, i].start()
    for copy in small[1:]:
        copy.wait()
    for i in range(layers):
        for j in range(PAIR):
            large[j, i].wait()
    scratch = sum_ref, power_ref, coupling_ref
    in_batches(vectors, lambda start, size: slabs_of(
        layers, parts, start, size, edge, ids_ref, other_ref, thick_ref, blocks_ref, decay_ref, outs, scratch))


def slabs_of(layers, parts, start, size, edge, ids_ref, other_ref, thick_ref, blocks_ref, decay_ref, outs, scratch):
    slab_d, slab_u, slab_ref, gap_ref, *onward = outs
    m = decay_ref.shape[-1]
    parity, top = ids_ref[1], ids_ref[2] == 0
    keys = [(k, j) for k in range(size) for j in range(PAIR)]
    factors = [1.0 + 0.5 * math.cos(2.0 * math.pi * i / parts) for i in range(parts)]
    segments = {}
    for k, j in keys:
        factor = pick(factors, (start + k) * PAIR + parity)
        for i in range(layers):
            thick = jnp.where(parity == j, thick_ref[i], other_ref[1, i])
            segments[k, j, i] = segment(factor, thick, [blocks_ref[j, i, b] for b in range(4)], decay_ref[...])
    slabs = {(k, j): segments[k, j, 0] for k, j in keys}
    for i in range(1, layers):
        couplings = [dot(slabs[k, j][3], segments[k, j, i][0]) for k, j in keys]
        gaps = inverses(couplings, 2, *scratch)
        for (k, j), gap in zip(keys, gaps):
            above, below = slabs[k, j], segments[k, j, i]
            by_d, by_u = inner_maps(above, below, gap)
            slab_d[start + k, j, i - 1, 0:m] = by_d[0]
            slab_d[start + k, j, i - 1, m:] = by_d[3]
            slab_u[start + k, j, i - 1, 0:m] = by_u[0]
            slab_u[start + k, j, i - 1, m:] = by_u[3]
            slabs[k, j] = (
                above[0] + dot(by_d[0], above[1]),
                dot(by_d[3], above[1]),
                dot(by_u[0], below[2]),
                below[3] + dot(by_u[3], below[2]),
            )
    for k, j in keys:
        for b in range(4):
            slab_ref[start + k, j, b] = slabs[k, j][b]
    couplings = [dot(slab_ref[start + k, 0, 3], slab_ref[start + k, 1, 0]) for k in range(size)]
    gaps = inverses(couplings, 2, *scratch)
    for k, gap in enumerate(gaps):
        gap_ref[start + k] = gap
        above, below = [[slab_ref[start + k, j, b] for b in range(4)] for j in range(PAIR)]
        if edge:
            first = dot(jnp.where(top, above[3], above[2]), jnp.where(top, below[2], below[0]))
            left = jnp.where(top, below[1], first)
            right = jnp.where(top, first, above[1])
            onward[0][start + k] = jnp.where(top, below[3], above[0]) + dot(left, dot(gap, right))


def maps_kernel(vectors, edge, ids_ref, slab_ref, gap_ref, *refs):
    pair_d, pair_u, *ends = refs[1:] if edge else refs
    m = gap_ref.shape[-1]
    top = ids_ref[2] == 0

    def maps_of(start, size):
        for k in range(size):
            k = start + k
            above = [slab_ref[k, 0, b] for b in range(4)]
            below = [slab_ref[k, 1, b] for b in range(4)]
            by_d, by_u = inner_maps(above, below, gap_ref[k])
            for r in range(4):
                pair_d[k, r * m:(r + 1) * m] = by_d[r]
                pair_u[k, r * m:(r + 1) * m] = by_u[r]
            if edge:
                inward = jnp.where(top, below[2], above[1])
                for r in range(4):
                    row = dot(jnp.where(top, by_u[r], by_d[r]), inward)
                    if r == 0:
                        row = row + jnp.where(top, 0.0, above[0])
                    if r == 3:
                        row = row + jnp.where(top, below[3], 0.0)
                    ends[0][k, r * m:(r + 1) * m] = row
            else:
                end_x, end_y = ends
                for r in range(4):
                    from_x, from_y = dot(by_d[r], above[1]), dot(by_u[r], below[2])
                    end_x[k, r * m:(r + 1) * m] = from_x + above[0] if r == 0 else from_x
                    end_y[k, r * m:(r + 1) * m] = from_y + below[3] if r == 3 else from_y

    in_batches(vectors, maps_of)


def pack_kernel(share, parts, ids_ref, drive_hbm, position_hbm, kind_hbm, thick_hbm, *outs):
    *blocks, described, held, drive_ref, position_ref, kind_ref, thick_ref, sems, drive_sems = outs
    layers = drive_hbm.shape[1]
    small = [
        pltpu.make_async_copy(position_hbm, position_ref, sems.at[0]),
        pltpu.make_async_copy(kind_hbm, kind_ref, sems.at[1]),
        pltpu.make_async_copy(thick_hbm, thick_ref, sems.at[2]),
    ]
    large = {
        (i, d): pltpu.make_async_copy(drive_hbm.at[0, i, d], drive_ref.at[i, d], drive_sems.at[i, d])
        for i in range(layers) for d in range(2)
    }
    for copy in [*small, *large.values()]:
        copy.start()
    for copy in small:
        copy.wait()
    cell = ids_ref[0]
    offset = jnp.abs(cell - position_ref[...])
    offset = jnp.minimum(offset, parts - offset)
    envelope = 1.0 / (1.0 + offset.astype(f32))
    for i in range(layers):
        described[0, i] = kind_ref[i].astype(f32)
        described[1, i] = thick_ref[i]
    for copy in large.values():
        copy.wait()
    for q in range(parts):
        span = slice(q * share, (q + 1) * share)
        held[q] = jnp.concatenate(
            [drive_ref[i, d, :, span] * envelope[:, span] for i in range(layers) for d in range(2)], axis=1
        )
    for step in range(parts):
        blocks[step][...] = held[cell ^ step]


def transform_kernel(parts, ids_ref, *refs):
    blocks, (_, kept, sent) = refs[:parts], refs[parts:]
    place, parity = ids_ref[0], ids_ref[1]
    loaded = [b[...] for b in blocks]
    cells = [place ^ step for step in range(parts)]
    for side, out in ((parity, kept), (1 - parity, sent)):
        for i in range(out.shape[0]):
            wave = PAIR * i + side
            total = cas(wave, cells[0], parts) * loaded[0]
            for step in range(1, parts):
                total = total + cas(wave, cells[step], parts) * loaded[step]
            out[i] = total


def sources_kernel(layers, share, vectors, edge, ids_ref, kept, got, slab_d, slab_u, pair_d, pair_u, slabs, *refs):
    m = kept.shape[1]
    parity, group = ids_ref[1], ids_ref[2]
    held = refs[-1]
    for k in range(vectors):
        held[parity, k] = kept[k]
        held[1 - parity, k] = got[k]
    ends = []
    for k in range(vectors):
        pair = []
        for j in range(PAIR):
            block = held[j, k]
            up, down = block[:, 0:share], block[:, share:2 * share]
            for i in range(1, layers):
                at = 2 * i * share
                up_b, down_b = block[:, at:at + share], block[:, at + share:at + 2 * share]
                both = dot(slab_d[k, j, i - 1], down) + dot(slab_u[k, j, i - 1], up_b)
                up, down = up + both[0:m], down_b + both[m:]
            slabs[k, 2 * j] = up
            slabs[k, 2 * j + 1] = down
            pair.append((up, down))
        if edge:
            rows = pl.ds(pl.multiple_of(jnp.where(group == 0, 3 * m, 0), 8), m)
            own = jnp.where(group == 0, pair[1][1], pair[0][0])
            ends.append(own + dot(pair_d[k, rows], pair[0][1]) + dot(pair_u[k, rows], pair[1][0]))
    if edge:
        refs[0][...] = jnp.concatenate(ends, axis=1)


def inner_kernel(vectors, slabs, pair_d, pair_u, inner):
    m = pair_d.shape[-1]
    for k in range(vectors):
        rows = dot(pair_d[k], slabs[k, 1]) + dot(pair_u[k], slabs[k, 2])
        inner[k, 0:m] = rows[0:m] + slabs[k, 0]
        inner[k, m:3 * m] = rows[m:3 * m]
        inner[k, 3 * m:] = rows[3 * m:] + slabs[k, 3]


def boundary_kernel(vectors, slabs, end, pair_d, pair_u, onward, arrived, inner, gap, bounced, sum_ref, power_ref, coupling_ref):
    share = slabs.shape[-1]
    inner_kernel(vectors, slabs, pair_d, pair_u, inner)
    bounced[...] = jnp.concatenate(
        [dot(arrived[k], end[:, k * share:(k + 1) * share]) for k in range(vectors)], axis=1
    )
    gaps = inverses([dot(arrived[k], onward[k]) for k in range(vectors)], 3, sum_ref, power_ref, coupling_ref)
    for k in range(vectors):
        gap[k] = gaps[k]


def fields_kernel(vectors, ids_ref, inner, answer, gap, bounced, crossed, kept, sent, held):
    m = inner.shape[1] // 4
    share = inner.shape[2]
    parity = ids_ref[1]
    inward = bounced[...] + crossed[...]
    for k in range(vectors):
        rows = inner[k] + dot(answer[k], dot(gap[k], inward[:, k * share:(k + 1) * share]))
        for j in range(PAIR):
            held[j, k] = jnp.concatenate([rows[2 * j * m:(2 * j + 1) * m], rows[(2 * j + 1) * m:(2 * j + 2) * m]], axis=1)
    for k in range(vectors):
        kept[k] = held[parity, k]
        sent[k] = held[1 - parity, k]


def return_kernel(parts, ids_ref, kept, got, *blocks):
    place, parity = ids_ref[0], ids_ref[1]
    vectors = kept.shape[0]
    mine, theirs = [kept[i] for i in range(vectors)], [got[i] for i in range(vectors)]
    for step in range(parts):
        cell = place ^ step
        total = None
        for side, fields in ((parity, mine), (1 - parity, theirs)):
            for i in range(vectors):
                term = cas(cell, PAIR * i + side, parts) * fields[i]
                total = term if total is None else total + term
        blocks[step][...] = total


def unpack_kernel(share, parts, ids_ref, *refs):
    blocks, (up, down, held) = refs[:parts], refs[parts:]
    place = ids_ref[0]
    for step in range(parts):
        held[place ^ step] = blocks[step][...]
    for side, out in enumerate((up, down)):
        span = slice(side * share, (side + 1) * share)
        out[0, 0] = jnp.concatenate([held[q][:, span] for q in range(parts)], axis=1)


def vmem():
    return pl.BlockSpec(memory_space=pltpu.VMEM)


def smem():
    return pl.BlockSpec(memory_space=pltpu.SMEM)


def call(kernel, scalars, arrays, shapes, scratch=(), flops=0, limit=12, after=(), small=(), far=()):
    moved = sum(a.size * 4 for a in (*arrays, *far)) + sum(math.prod(s) * 4 for s in shapes)
    return pl.pallas_call(
        kernel,
        out_shape=tuple(jax.ShapeDtypeStruct(s, f32) for s in (*shapes, *small)),
        in_specs=[smem()] * len(scalars)
        + [vmem()] * len(arrays)
        + [pl.BlockSpec(memory_space=pltpu.HBM)] * len(far)
        + [pl.BlockSpec(memory_space=pl.ANY)] * len(after),
        out_specs=tuple([vmem()] * len(shapes) + [smem()] * len(small)),
        scratch_shapes=[pltpu.VMEM(s, f32) if isinstance(s, tuple) else s for s in scratch],
        cost_estimate=pl.CostEstimate(flops=flops, bytes_accessed=moved, transcendentals=0),
        compiler_params=pltpu.CompilerParams(vmem_limit_bytes=limit << 20),
    )(*scalars, *arrays, *(pltpu.with_memory_space_constraint(a, pltpu.HBM) for a in far), *after)


def exact(left_side, right_side):
    return jnp.einsum("kij,kjl->kil", left_side, right_side, precision=lax.Precision.HIGHEST)


def plain_inverse(coupling):
    identity = jnp.eye(coupling.shape[-1], dtype=f32)

    def step(_, approx):
        return exact(approx, 2.0 * identity - exact(identity - coupling, approx))

    return lax.fori_loop(0, 6, step, identity + coupling)


def chain(groups, group, depth, end_x, end_y, inner):
    m = end_x.shape[-1]
    down_route = [(i, i + PAIR) for i in range(depth - PAIR)]
    up_route = [(i + PAIR, i) for i in range(depth - PAIR)]
    top_t, down_t = end_x[:, 0:m], end_x[:, 3 * m:]
    up_t, end_t = end_y[:, 0:m], end_y[:, 3 * m:]
    top_s, end_s = inner[:, 0:m], inner[:, 3 * m:]

    def turn_of(turn, carry):
        prefix, suffix, falling, rising = carry
        from_above = [lax.ppermute(f, "stack", down_route) for f in falling]
        from_below = [lax.ppermute(r, "stack", up_route) for r in rising]
        prefix = [jnp.where(group == turn, new, old) for new, old in zip(from_above, prefix)]
        suffix = [jnp.where(group == groups - 1 - turn, new, old) for new, old in zip(from_below, suffix)]
        carry_d = exact(down_t, plain_inverse(exact(prefix[0], top_t)))
        carry_u = exact(up_t, plain_inverse(exact(suffix[0], end_t)))
        grown_d = [end_t + exact(carry_d, exact(prefix[0], up_t)), end_s + exact(carry_d, prefix[1] + exact(prefix[0], top_s))]
        grown_u = [top_t + exact(carry_u, exact(suffix[0], down_t)), top_s + exact(carry_u, suffix[1] + exact(suffix[0], end_s))]
        falling = [jnp.where(group == turn, new, old) for new, old in zip(grown_d, falling)]
        rising = [jnp.where(group == groups - 1 - turn, new, old) for new, old in zip(grown_u, rising)]
        return prefix, suffix, falling, rising

    nothing = [jnp.zeros_like(end_t), jnp.zeros_like(end_s)]
    prefix, suffix, _, _ = lax.fori_loop(1, groups, turn_of, (nothing, nothing, [end_t, end_s], [top_t, top_s]))
    lower = plain_inverse(exact(suffix[0], end_t))
    below = suffix[1] + exact(suffix[0], end_s)
    top_all = top_t + exact(up_t, exact(lower, exact(suffix[0], down_t)))
    source_all = top_s + exact(up_t, exact(lower, below))
    in_x = exact(plain_inverse(exact(prefix[0], top_all)), prefix[1] + exact(prefix[0], source_all))
    in_y = exact(lower, below + exact(suffix[0], exact(down_t, in_x)))
    return inner + exact(end_x, in_x) + exact(end_y, in_y)


def shards(drive, positions, materials, table, thickness, decay):
    parts = lax.axis_size("bloch")
    depth = lax.axis_size("stack")
    groups = depth // PAIR
    edge = groups == 2
    layers, m, columns = drive.shape[1], drive.shape[3], drive.shape[4]
    vectors = parts // PAIR
    share = columns // parts
    width = layers * 2 * share
    assert drive.shape[0] == 1 and depth % PAIR == 0 and columns % parts == 0
    assert parts % PAIR == 0 and parts & (parts - 1) == 0
    stack_index = lax.axis_index("stack")
    group, parity = stack_index // PAIR, stack_index % PAIR
    ids = jnp.stack([lax.axis_index("bloch"), parity, group]).astype(jnp.int32)
    partner = [(i, i ^ 1) for i in range(depth)]
    across = [(i, i + PAIR) for i in range(depth - PAIR)] + [(i + PAIR, i) for i in range(depth - PAIR)]
    dma = pltpu.SemaphoreType.DMA

    def deal(blocks):
        out = {0: blocks[0]}
        for step in sorted(range(1, parts), reverse=True):
            out[step] = lax.ppermute(blocks[step], "bloch", [(i, i ^ step) for i in range(parts)])
        return [out[step] for step in range(parts)]

    *packed, described = call(
        functools.partial(pack_kernel, share, parts),
        [ids], [], [(m, width)] * parts,
        [(parts, m, width), (layers, 2, m, columns), pltpu.VMEM((1, columns), jnp.int32), pltpu.SMEM((layers,), jnp.int32),
         pltpu.SMEM((layers,), f32), dma((3,)), dma((layers, 2))],
        small=[(2, layers)], far=[drive, positions[None, :], materials, thickness],
    )
    other = lax.ppermute(described, "stack", partner)
    arrived = deal(packed)

    squares = [(vectors * PAIR, m, m)] * 3
    slab_d, slab_u, slab, gap, *onward = call(
        functools.partial(slabs_kernel, layers, vectors, parts, edge),
        [ids, other], [],
        [(vectors, PAIR, layers - 1, 2 * m, m)] * 2 + [(vectors, PAIR, 4, m, m), (vectors, m, m)] + [(vectors, m, m)] * edge,
        squares + [pltpu.SMEM((layers,), jnp.int32), pltpu.SMEM((layers,), f32), (PAIR, layers, 4, m, m), (1, m),
                   dma((3,)), dma((PAIR, layers))],
        3000 * m**3, 32, far=[materials, thickness, table, decay[None, :]],
    )
    if edge:
        opposite = lax.ppermute(onward[0], "stack", across)
    pair_d, pair_u, *ends = call(
        functools.partial(maps_kernel, vectors, edge),
        [ids], [slab, gap], [(vectors, 4 * m, m)] * (3 if edge else 4), (), 500 * m**3, after=onward,
    )

    kept, sent = call(
        functools.partial(transform_kernel, parts),
        [ids], arrived, [(vectors, m, width)] * 2, (), after=[pair_d],
    )
    got = lax.ppermute(sent, "stack", partner)
    slabs, *end = call(
        functools.partial(sources_kernel, layers, share, vectors, edge),
        [ids], [kept, got, slab_d, slab_u, pair_d, pair_u],
        [(vectors, 4, m, share)] + ([(m, vectors * share)] if edge else []),
        [(PAIR, vectors, m, width)],
    )
    if edge:
        crossed = lax.ppermute(end[0], "stack", across)
        inner, gate, bounced = call(
            functools.partial(boundary_kernel, vectors),
            [], [slabs, end[0], pair_d, pair_u, onward[0], opposite],
            [(vectors, 4 * m, share), (vectors, m, m), (m, vectors * share)], squares, 1000 * m**3,
        )
        kept, sent = call(
            functools.partial(fields_kernel, vectors),
            [ids], [inner, ends[0], gate, bounced, crossed],
            [(vectors, m, 2 * share)] * 2, [(PAIR, vectors, m, 2 * share)],
        )
    else:
        (inner,) = call(
            functools.partial(inner_kernel, vectors), [], [slabs, pair_d, pair_u], [(vectors, 4 * m, share)], (),
        )
        rows = chain(groups, group, depth, ends[0], ends[1], inner)
        sides = [jnp.concatenate([rows[:, 2 * j * m:(2 * j + 1) * m], rows[:, (2 * j + 1) * m:(2 * j + 2) * m]], 2) for j in range(PAIR)]
        kept = jnp.where(parity == 0, sides[0], sides[1])
        sent = jnp.where(parity == 0, sides[1], sides[0])
    got = lax.ppermute(sent, "stack", partner)

    blocks = call(functools.partial(return_kernel, parts), [ids], [kept, got], [(m, 2 * share)] * parts, ())
    blocks = deal(blocks)
    return call(
        functools.partial(unpack_kernel, share, parts),
        [ids], blocks, [(1, 1, m, columns)] * 2, [(parts, m, 2 * share)],
    )


def solution(mesh):
    in_specs = (
        P(("groups", "bloch"), "stack", None, None, None),
        P("groups"),
        P(("groups", "stack")),
        P(),
        P(("groups", "stack")),
        P(),
    )
    out_specs = (
        P(("groups", "bloch"), "stack", None, None),
        P(("groups", "bloch"), "stack", None, None),
    )

    return jax.shard_map(shards, mesh=mesh, in_specs=in_specs, out_specs=out_specs, check_vma=False)
```

```python
import functools
import math

import jax
import jax.numpy as jnp
from jax import lax
from jax.experimental import pallas as pl
from jax.experimental.pallas import tpu as pltpu
from jax.sharding import PartitionSpec as P

PAIR = 2
NEGLIGIBLE = 4e-6

f32 = jnp.float32


def dot(left_side, right_side, precision=lax.Precision.HIGH):
    return lax.dot_general(
        left_side,
        right_side,
        (((1,), (0,)), ((), ())),
        precision=precision,
        preferred_element_type=f32,
    )


def eye(size):
    rows = lax.broadcasted_iota(jnp.int32, (size, size), 0)
    columns = lax.broadcasted_iota(jnp.int32, (size, size), 1)
    return (rows == columns).astype(f32)


def inverses(couplings, doublings, sum_ref, power_ref, coupling_ref):
    size = couplings[0].shape[0]
    count = len(couplings)
    identity = eye(size)
    sums = [identity + c for c in couplings]
    powers = [dot(c, c) for c in couplings]
    for turn in range(doublings):
        sums = [s + dot(s, p) for s, p in zip(sums, powers)]
        if turn < doublings - 1:
            powers = [dot(p, p) for p in powers]
    largest = functools.reduce(jnp.maximum, [jnp.sum(p * p, axis=0, keepdims=True) for p in powers])
    for i, (s, p, c) in enumerate(zip(sums, powers, couplings)):
        sum_ref[i] = s
        power_ref[i] = p
        coupling_ref[i] = c

    @pl.when(jnp.logical_not(jnp.sum(largest) <= NEGLIGIBLE))
    def _():
        exact = lax.Precision.HIGHEST

        def one(i, carry):
            def going(state):
                step, left_over = state
                return (step < 16) & (left_over > NEGLIGIBLE) & (left_over < 1e12)

            def double(state):
                step, _ = state
                power = dot(power_ref[i], power_ref[i], exact)
                power_ref[i] = power
                sum_ref[i] = sum_ref[i] + dot(sum_ref[i], power, exact)
                return (step + 1, jnp.sum(power * power))

            start = power_ref[i]
            _, left_over = lax.while_loop(going, double, (jnp.int32(0), jnp.sum(start * start)))

            @pl.when(jnp.logical_not(left_over <= NEGLIGIBLE))
            def _():
                system = eye(size) - coupling_ref[i]
                flipped = lax.dot_general(
                    system,
                    eye(size),
                    (((0,), (0,)), ((), ())),
                    precision=exact,
                    preferred_element_type=f32,
                )
                row_bound = jnp.max(jnp.sum(jnp.abs(system), axis=1, keepdims=True))
                column_bound = jnp.max(jnp.sum(jnp.abs(system), axis=0, keepdims=True))
                sum_ref[i] = flipped / (row_bound * column_bound)

                def refining(state):
                    step, gap = state
                    return (step < 100) & (gap > 1e-4)

                def refine(state):
                    step, _ = state
                    error = eye(size) - dot(eye(size) - coupling_ref[i], sum_ref[i], exact)
                    sum_ref[i] = sum_ref[i] + dot(sum_ref[i], error, exact)
                    return (step + 1, jnp.max(jnp.abs(error)))

                lax.while_loop(refining, refine, (jnp.int32(0), f32(1.0)))

            return carry

        lax.fori_loop(0, count, one, 0)

    return [sum_ref[i] for i in range(count)]


def inner_maps(above, below, gap):
    _, _, up_a, bottom_a = above
    top_b, down_b, _, _ = below
    identity = eye(gap.shape[0])
    mid_y_d = dot(top_b, gap)
    mid_x_u = dot(gap, bottom_a)
    mid_y_u = identity + dot(top_b, mid_x_u)
    return (
        (dot(up_a, mid_y_d), gap, mid_y_d, dot(down_b, gap)),
        (dot(up_a, mid_y_u), mid_x_u, mid_y_u, dot(down_b, mid_x_u)),
    )


def in_batches(count, work):
    size = 2 if count % 2 == 0 else 1
    if count == size:
        work(0, size)
    else:
        def step(i, carry):
            work(i * size, size)
            return carry

        lax.fori_loop(0, count // size, step, 0)


def pick(values, index):
    value = f32(values[0])
    for i in range(1, len(values)):
        value = jnp.where(index == i, f32(values[i]), value)
    return value


def cas(row, column, count):
    angles = [2.0 * math.pi * i / count for i in range(count)]
    return pick([(math.cos(a) + math.sin(a)) / math.sqrt(count) for a in angles], lax.rem(row * column, count))


def segment(factor, thick, blocks, decay):
    m = decay.shape[-1]
    row = jnp.exp(-(thick * factor) * decay)
    column = jnp.sum(eye(m) * row, axis=1, keepdims=True)
    return tuple(column * blocks[b] * row for b in range(4))


def slabs_kernel(layers, vectors, parts, edge, ids_ref, other_ref, table_ref, kind_hbm, thick_hbm, decay_hbm, *refs):
    *outs, sum_ref, power_ref, coupling_ref, kind_ref, thick_ref, decay_ref, sems = refs
    small = [
        pltpu.make_async_copy(kind_hbm, kind_ref, sems.at[0]),
        pltpu.make_async_copy(thick_hbm, thick_ref, sems.at[1]),
        pltpu.make_async_copy(decay_hbm, decay_ref, sems.at[2]),
    ]
    for copy in small:
        copy.start()
    for copy in small:
        copy.wait()
    scratch = sum_ref, power_ref, coupling_ref
    in_batches(vectors, lambda start, size: slabs_of(
        layers, parts, start, size, edge, ids_ref, other_ref, kind_ref, thick_ref, table_ref, decay_ref, outs, scratch))


def slabs_of(layers, parts, start, size, edge, ids_ref, other_ref, kind_ref, thick_ref, table_ref, decay_ref, outs, scratch):
    slab_d, slab_u, slab_ref, gap_ref, *edges = outs
    if edge:
        onward, end_d, end_u = edges
    m = decay_ref.shape[-1]
    parity, top = ids_ref[1], ids_ref[2] == 0
    keys = [(k, j) for k in range(size) for j in range(PAIR)]
    factors = [1.0 + 0.5 * math.cos(2.0 * math.pi * i / parts) for i in range(parts)]
    segments = {}
    for k, j in keys:
        factor = pick(factors, (start + k) * PAIR + parity)
        for i in range(layers):
            kind = jnp.where(parity == j, kind_ref[i], other_ref[0, i].astype(jnp.int32))
            thick = jnp.where(parity == j, thick_ref[i], other_ref[1, i])
            segments[k, j, i] = segment(factor, thick, [table_ref[kind, b] for b in range(4)], decay_ref[...])
    slabs = {(k, j): segments[k, j, 0] for k, j in keys}
    for i in range(1, layers):
        couplings = [dot(slabs[k, j][3], segments[k, j, i][0]) for k, j in keys]
        gaps = inverses(couplings, 2, *scratch)
        for (k, j), gap in zip(keys, gaps):
            above, below = slabs[k, j], segments[k, j, i]
            by_d, by_u = inner_maps(above, below, gap)
            slab_d[start + k, j, i - 1, 0:m] = by_d[0]
            slab_d[start + k, j, i - 1, m:] = by_d[3]
            slab_u[start + k, j, i - 1, 0:m] = by_u[0]
            slab_u[start + k, j, i - 1, m:] = by_u[3]
            slabs[k, j] = (
                above[0] + dot(by_d[0], above[1]),
                dot(by_d[3], above[1]),
                dot(by_u[0], below[2]),
                below[3] + dot(by_u[3], below[2]),
            )
    for k, j in keys:
        for b in range(4):
            slab_ref[start + k, j, b] = slabs[k, j][b]
    couplings = [dot(slab_ref[start + k, 0, 3], slab_ref[start + k, 1, 0]) for k in range(size)]
    gaps = inverses(couplings, 2, *scratch)
    for k, gap in enumerate(gaps):
        gap_ref[start + k] = gap
        above, below = [[slab_ref[start + k, j, b] for b in range(4)] for j in range(PAIR)]
        if edge:
            first = dot(jnp.where(top, above[3], above[2]), jnp.where(top, below[2], below[0]))
            left = jnp.where(top, below[1], first)
            right = jnp.where(top, first, above[1])
            through = dot(left, gap)
            onward[start + k] = jnp.where(top, below[3], above[0]) + dot(through, right)
            end_d[start + k] = through
            end_u[start + k] = dot(through, above[3]) + jnp.where(top, 0.0, above[2])


def maps_kernel(vectors, edge, ids_ref, slab_ref, gap_ref, *refs):
    pair_d, pair_u, *ends = refs[1:] if edge else refs
    m = gap_ref.shape[-1]
    top = ids_ref[2] == 0

    def maps_of(start, size):
        for k in range(size):
            k = start + k
            above = [slab_ref[k, 0, b] for b in range(4)]
            below = [slab_ref[k, 1, b] for b in range(4)]
            by_d, by_u = inner_maps(above, below, gap_ref[k])
            for r in range(4):
                pair_d[k, r * m:(r + 1) * m] = by_d[r]
                pair_u[k, r * m:(r + 1) * m] = by_u[r]
            if edge:
                inward = jnp.where(top, below[2], above[1])
                for r in range(4):
                    row = dot(jnp.where(top, by_u[r], by_d[r]), inward)
                    if r == 0:
                        row = row + jnp.where(top, 0.0, above[0])
                    if r == 3:
                        row = row + jnp.where(top, below[3], 0.0)
                    ends[0][k, r * m:(r + 1) * m] = row
            else:
                end_x, end_y = ends
                for r in range(4):
                    from_x, from_y = dot(by_d[r], above[1]), dot(by_u[r], below[2])
                    end_x[k, r * m:(r + 1) * m] = from_x + above[0] if r == 0 else from_x
                    end_y[k, r * m:(r + 1) * m] = from_y + below[3] if r == 3 else from_y

    in_batches(vectors, maps_of)


def pack_kernel(share, parts, ids_ref, drive_hbm, position_hbm, kind_hbm, thick_hbm, *outs):
    *blocks, described, drive_ref, position_ref, kind_ref, thick_ref, sems, drive_sems = outs
    layers = drive_hbm.shape[1]
    small = [
        pltpu.make_async_copy(position_hbm, position_ref, sems.at[0]),
        pltpu.make_async_copy(kind_hbm, kind_ref, sems.at[1]),
        pltpu.make_async_copy(thick_hbm, thick_ref, sems.at[2]),
    ]
    large = {
        (i, d): pltpu.make_async_copy(drive_hbm.at[0, i, d], drive_ref.at[i, d], drive_sems.at[i, d])
        for i in range(layers) for d in range(2)
    }
    for copy in [*small, *large.values()]:
        copy.start()
    for copy in small:
        copy.wait()
    cell = ids_ref[0]
    offset = jnp.abs(cell - position_ref[...])
    offset = jnp.minimum(offset, parts - offset)
    envelope = 1.0 / (1.0 + offset.astype(f32))
    for i in range(layers):
        described[0, i] = kind_ref[i].astype(f32)
        described[1, i] = thick_ref[i]
    for i in range(layers):
        for d in range(2):
            large[i, d].wait()
        loaded = [drive_ref[i, d] * envelope for d in range(2)]
        for here in range(parts):
            @pl.when(cell == here)
            def _():
                for step in range(parts):
                    q = here ^ step
                    blocks[step][:, 2 * i * share:2 * (i + 1) * share] = jnp.concatenate(
                        [side[:, q * share:(q + 1) * share] for side in loaded], axis=1
                    )


def transformed(blocks, ids_ref, side, parts):
    place = ids_ref[0]
    loaded = [b[...] for b in blocks]
    cells = [place ^ step for step in range(parts)]
    for i in range(parts // PAIR):
        wave = PAIR * i + side
        total = cas(wave, cells[0], parts) * loaded[0]
        for step in range(1, parts):
            total = total + cas(wave, cells[step], parts) * loaded[step]
        yield total


def transform_kernel(parts, ids_ref, *refs):
    blocks, sent = refs[:parts], refs[-1]
    for i, total in enumerate(transformed(blocks, ids_ref, 1 - ids_ref[1], parts)):
        sent[i] = total


def through_slab(layers, share, block, k, j, slab_d, slab_u):
    m = block.shape[0]
    up, down = block[:, 0:share], block[:, share:2 * share]
    for i in range(1, layers):
        at = 2 * i * share
        up_b, down_b = block[:, at:at + share], block[:, at + share:at + 2 * share]
        both = dot(slab_d[k, j, i - 1], down) + dot(slab_u[k, j, i - 1], up_b)
        up, down = up + both[0:m], down_b + both[m:]
    return up, down


def near_kernel(layers, share, parts, ids_ref, *refs):
    blocks, (slab_d, slab_u, near) = refs[:parts], refs[parts:]
    parity = ids_ref[1]
    for k, block in enumerate(transformed(blocks, ids_ref, parity, parts)):
        near[k, 0], near[k, 1] = through_slab(layers, share, block, k, parity, slab_d, slab_u)


def far_kernel(layers, share, vectors, edge, ids_ref, near, got, slab_d, slab_u, *refs):
    parity, top = ids_ref[1], ids_ref[2] == 0
    slabs = refs[2] if edge else refs[0]
    for k in range(vectors):
        up, down = through_slab(layers, share, got[k], k, 1 - parity, slab_d, slab_u)
        slabs[k, 2 * parity] = near[k, 0]
        slabs[k, 2 * parity + 1] = near[k, 1]
        slabs[k, 2 * (1 - parity)] = up
        slabs[k, 2 * (1 - parity) + 1] = down
    if edge:
        end_d, end_u, _, end = refs
        ends = []
        for k in range(vectors):
            own = jnp.where(top, slabs[k, 3], slabs[k, 0])
            ends.append(own + dot(end_d[k], slabs[k, 1]) + dot(end_u[k], slabs[k, 2]))
        end[...] = jnp.concatenate(ends, axis=1)


def inner_kernel(vectors, slabs, pair_d, pair_u, inner):
    m = pair_d.shape[-1]
    for k in range(vectors):
        rows = dot(pair_d[k], slabs[k, 1]) + dot(pair_u[k], slabs[k, 2])
        inner[k, 0:m] = rows[0:m] + slabs[k, 0]
        inner[k, m:3 * m] = rows[m:3 * m]
        inner[k, 3 * m:] = rows[3 * m:] + slabs[k, 3]


def boundary_kernel(vectors, slabs, end, pair_d, pair_u, onward, arrived, inner, gap, bounced, sum_ref, power_ref, coupling_ref):
    share = slabs.shape[-1]
    inner_kernel(vectors, slabs, pair_d, pair_u, inner)
    bounced[...] = jnp.concatenate(
        [dot(arrived[k], end[:, k * share:(k + 1) * share]) for k in range(vectors)], axis=1
    )
    gaps = inverses([dot(arrived[k], onward[k]) for k in range(vectors)], 3, sum_ref, power_ref, coupling_ref)
    for k in range(vectors):
        gap[k] = gaps[k]


def rows_of(j, k, inner, answer, inward):
    m = inner.shape[1] // 4
    rows = pl.ds(pl.multiple_of(2 * j * m, 8), 2 * m)
    both = inner[k, rows] + dot(answer[k, rows], inward)
    return jnp.concatenate([both[0:m], both[m:]], axis=1)


def sent_kernel(vectors, ids_ref, inner, answer, gate, bounced, crossed, sent, inward_ref):
    share = inner.shape[2]
    inward = bounced[...] + crossed[...]
    for k in range(vectors):
        value = dot(gate[k], inward[:, k * share:(k + 1) * share])
        inward_ref[k] = value
        sent[k] = rows_of(1 - ids_ref[1], k, inner, answer, value)


def kept_kernel(vectors, ids_ref, inner, answer, inward_ref, kept):
    for k in range(vectors):
        kept[k] = rows_of(ids_ref[1], k, inner, answer, inward_ref[k])


def return_kernel(parts, ids_ref, kept, got, *blocks):
    place, parity = ids_ref[0], ids_ref[1]
    vectors = kept.shape[0]
    mine, theirs = [kept[i] for i in range(vectors)], [got[i] for i in range(vectors)]
    for step in range(parts):
        cell = place ^ step
        total = None
        for side, fields in ((parity, mine), (1 - parity, theirs)):
            for i in range(vectors):
                term = cas(cell, PAIR * i + side, parts) * fields[i]
                total = term if total is None else total + term
        blocks[step][...] = total


def unpack_kernel(share, parts, ids_ref, *refs):
    blocks, outs = refs[:parts], refs[parts:]
    for here in range(parts):
        @pl.when(ids_ref[0] == here)
        def _():
            for side, out in enumerate(outs):
                span = slice(side * share, (side + 1) * share)
                out[0, 0] = jnp.concatenate([blocks[here ^ q][:, span] for q in range(parts)], axis=1)


def vmem():
    return pl.BlockSpec(memory_space=pltpu.VMEM)


def smem():
    return pl.BlockSpec(memory_space=pltpu.SMEM)


def call(kernel, scalars, arrays, shapes, scratch=(), flops=0, limit=12, after=(), small=(), far=()):
    moved = sum(a.size * 4 for a in (*arrays, *far)) + sum(math.prod(s) * 4 for s in shapes)
    return pl.pallas_call(
        kernel,
        out_shape=tuple(jax.ShapeDtypeStruct(s, f32) for s in (*shapes, *small)),
        in_specs=[smem()] * len(scalars)
        + [vmem()] * len(arrays)
        + [pl.BlockSpec(memory_space=pltpu.HBM)] * len(far)
        + [pl.BlockSpec(memory_space=pl.ANY)] * len(after),
        out_specs=tuple([vmem()] * len(shapes) + [smem()] * len(small)),
        scratch_shapes=[pltpu.VMEM(s, f32) if isinstance(s, tuple) else s for s in scratch],
        cost_estimate=pl.CostEstimate(flops=flops, bytes_accessed=moved, transcendentals=0),
        compiler_params=pltpu.CompilerParams(vmem_limit_bytes=limit << 20),
    )(*scalars, *arrays, *(pltpu.with_memory_space_constraint(a, pltpu.HBM) for a in far), *after)


def exact(left_side, right_side):
    return jnp.einsum("kij,kjl->kil", left_side, right_side, precision=lax.Precision.HIGHEST)


def plain_inverse(coupling):
    identity = jnp.eye(coupling.shape[-1], dtype=f32)

    def step(_, approx):
        return exact(approx, 2.0 * identity - exact(identity - coupling, approx))

    return lax.fori_loop(0, 6, step, identity + coupling)


def chain(groups, group, depth, end_x, end_y, inner):
    m = end_x.shape[-1]
    down_route = [(i, i + PAIR) for i in range(depth - PAIR)]
    up_route = [(i + PAIR, i) for i in range(depth - PAIR)]
    top_t, down_t = end_x[:, 0:m], end_x[:, 3 * m:]
    up_t, end_t = end_y[:, 0:m], end_y[:, 3 * m:]
    top_s, end_s = inner[:, 0:m], inner[:, 3 * m:]

    def turn_of(turn, carry):
        prefix, suffix, falling, rising = carry
        from_above = [lax.ppermute(f, "stack", down_route) for f in falling]
        from_below = [lax.ppermute(r, "stack", up_route) for r in rising]
        prefix = [jnp.where(group == turn, new, old) for new, old in zip(from_above, prefix)]
        suffix = [jnp.where(group == groups - 1 - turn, new, old) for new, old in zip(from_below, suffix)]
        carry_d = exact(down_t, plain_inverse(exact(prefix[0], top_t)))
        carry_u = exact(up_t, plain_inverse(exact(suffix[0], end_t)))
        grown_d = [end_t + exact(carry_d, exact(prefix[0], up_t)), end_s + exact(carry_d, prefix[1] + exact(prefix[0], top_s))]
        grown_u = [top_t + exact(carry_u, exact(suffix[0], down_t)), top_s + exact(carry_u, suffix[1] + exact(suffix[0], end_s))]
        falling = [jnp.where(group == turn, new, old) for new, old in zip(grown_d, falling)]
        rising = [jnp.where(group == groups - 1 - turn, new, old) for new, old in zip(grown_u, rising)]
        return prefix, suffix, falling, rising

    nothing = [jnp.zeros_like(end_t), jnp.zeros_like(end_s)]
    prefix, suffix, _, _ = lax.fori_loop(1, groups, turn_of, (nothing, nothing, [end_t, end_s], [top_t, top_s]))
    lower = plain_inverse(exact(suffix[0], end_t))
    below = suffix[1] + exact(suffix[0], end_s)
    top_all = top_t + exact(up_t, exact(lower, exact(suffix[0], down_t)))
    source_all = top_s + exact(up_t, exact(lower, below))
    in_x = exact(plain_inverse(exact(prefix[0], top_all)), prefix[1] + exact(prefix[0], source_all))
    in_y = exact(lower, below + exact(suffix[0], exact(down_t, in_x)))
    return inner + exact(end_x, in_x) + exact(end_y, in_y)


def shards(drive, positions, materials, table, thickness, decay):
    parts = lax.axis_size("bloch")
    depth = lax.axis_size("stack")
    groups = depth // PAIR
    edge = groups == 2
    layers, m, columns = drive.shape[1], drive.shape[3], drive.shape[4]
    vectors = parts // PAIR
    share = columns // parts
    width = layers * 2 * share
    assert drive.shape[0] == 1 and depth % PAIR == 0 and columns % parts == 0
    assert parts % PAIR == 0 and parts & (parts - 1) == 0
    stack_index = lax.axis_index("stack")
    group, parity = stack_index // PAIR, stack_index % PAIR
    ids = jnp.stack([lax.axis_index("bloch"), parity, group]).astype(jnp.int32)
    partner = [(i, i ^ 1) for i in range(depth)]
    across = [(i, i + PAIR) for i in range(depth - PAIR)] + [(i + PAIR, i) for i in range(depth - PAIR)]
    dma = pltpu.SemaphoreType.DMA

    def deal(blocks):
        out = {0: blocks[0]}
        for step in sorted(range(1, parts), reverse=True):
            out[step] = lax.ppermute(blocks[step], "bloch", [(i, i ^ step) for i in range(parts)])
        return [out[step] for step in range(parts)]

    *packed, described = call(
        functools.partial(pack_kernel, share, parts),
        [ids], [], [(m, width)] * parts,
        [(layers, 2, m, columns), pltpu.VMEM((1, columns), jnp.int32), pltpu.SMEM((layers,), jnp.int32),
         pltpu.SMEM((layers,), f32), dma((3,)), dma((layers, 2))],
        1000 * m**3, small=[(2, layers)], far=[drive, positions[None, :], materials, thickness],
    )
    other = lax.ppermute(described, "stack", partner)
    arrived = deal(packed)

    squares = [(vectors * PAIR, m, m)] * 3
    slab_d, slab_u, slab, gap, *edges = call(
        functools.partial(slabs_kernel, layers, vectors, parts, edge),
        [ids, other], [table],
        [(vectors, PAIR, layers - 1, 2 * m, m)] * 2 + [(vectors, PAIR, 4, m, m), (vectors, m, m)] + [(vectors, m, m)] * (3 * edge),
        squares + [pltpu.SMEM((layers,), jnp.int32), pltpu.SMEM((layers,), f32), (1, m), dma((3,))],
        3000 * m**3, 32, far=[materials, thickness, decay[None, :]],
    )
    if edge:
        opposite = lax.ppermute(edges[0], "stack", across)

    (sent,) = call(functools.partial(transform_kernel, parts), [ids], arrived, [(vectors, m, width)], (), after=[gap])
    got = lax.ppermute(sent, "stack", partner)
    (near,) = call(
        functools.partial(near_kernel, layers, share, parts),
        [ids], [*arrived, slab_d, slab_u], [(vectors, 2, m, share)], (),
    )
    slabs, *end = call(
        functools.partial(far_kernel, layers, share, vectors, edge),
        [ids], [near, got, slab_d, slab_u, *edges[1:]],
        [(vectors, 4, m, share)] + [(m, vectors * share)] * edge, (),
    )
    pair_d, pair_u, *ends = call(
        functools.partial(maps_kernel, vectors, edge),
        [ids], [slab, gap], [(vectors, 4 * m, m)] * (3 if edge else 4), (), 500 * m**3, after=end,
    )
    if edge:
        crossed = lax.ppermute(end[0], "stack", across)
        inner, gate, bounced = call(
            functools.partial(boundary_kernel, vectors),
            [], [slabs, end[0], pair_d, pair_u, edges[0], opposite],
            [(vectors, 4 * m, share), (vectors, m, m), (m, vectors * share)], squares, 1000 * m**3,
        )
        sent, inward = call(
            functools.partial(sent_kernel, vectors), [ids], [inner, ends[0], gate, bounced, crossed],
            [(vectors, m, 2 * share), (vectors, m, share)], (),
        )
    else:
        (inner,) = call(
            functools.partial(inner_kernel, vectors), [], [slabs, pair_d, pair_u], [(vectors, 4 * m, share)], (),
        )
        rows = chain(groups, group, depth, ends[0], ends[1], inner)
        sides = [jnp.concatenate([rows[:, 2 * j * m:(2 * j + 1) * m], rows[:, (2 * j + 1) * m:(2 * j + 2) * m]], 2) for j in range(PAIR)]
        sent = jnp.where(parity == 0, sides[1], sides[0])
    got = lax.ppermute(sent, "stack", partner)
    if edge:
        (kept,) = call(
            functools.partial(kept_kernel, vectors), [ids], [inner, ends[0], inward], [(vectors, m, 2 * share)], (),
        )
    else:
        kept = jnp.where(parity == 0, sides[0], sides[1])

    blocks = call(functools.partial(return_kernel, parts), [ids], [kept, got], [(m, 2 * share)] * parts, ())
    blocks = deal(blocks)
    return call(
        functools.partial(unpack_kernel, share, parts),
        [ids], blocks, [(1, 1, m, columns)] * 2, (),
    )


def solution(mesh):
    in_specs = (
        P(("groups", "bloch"), "stack", None, None, None),
        P("groups"),
        P(("groups", "stack")),
        P(),
        P(("groups", "stack")),
        P(),
    )
    out_specs = (
        P(("groups", "bloch"), "stack", None, None),
        P(("groups", "bloch"), "stack", None, None),
    )

    return jax.shard_map(shards, mesh=mesh, in_specs=in_specs, out_specs=out_specs, check_vma=False)
```
